512 devices in a mesh: tok: 64 (over z, y_hi, x), feat: 8 (over y_lo, core).
Axes of the slice: x: 4, y: 8 (y_hi: 2, y_lo: 4; y = y_hi * 4 + y_lo), z: 8, core: 2. Of those that a mesh axis runs over, the one named last changes fastest.
Arguments:
- activations: bfloat16 [131072, 8192], P('tok', 'feat')
- labels: int32 [131072], P('tok'), may hold values from 0 to 7, as said below
Outputs:
- cov_panel: float32 [1024, 8192], P('tok', 'feat')
- cross_cov: float32 [8, 8192], P(None, 'feat')
The draws below stay inside these ranges and needn't reach their ends.
Inputs may be any that keep to these rules, and one draw needn't show every extreme that they name: `labels`: each token's class.
All inputs are finite; a program needn't handle non-finite values.
Results may differ from the reference program's by a relative error of at most 0.0017.
Values may be sent and summed in bfloat16 or wider, within the bound.
A program may use at most 64 MiB of HBM per device.

```python
import jax
import jax.numpy as jnp
from jax import lax

D = 8192
CLASSES = 8
PANEL = 128
TOK_DEV = 2048
TOKENS = 131072
N_TOK = 64
N_FEAT = 8


def shared_labels(key):
    return jax.random.randint(jax.random.fold_in(key, 11), (TOKENS,), 0, CLASSES).astype(jnp.int32)


def draw_labels(key, part):
    return shared_labels(key)


def draw_activations(key, part):
    classes = shared_labels(key)
    latent_count = 512
    offset = 1.5 * jax.random.normal(jax.random.fold_in(key, 12), (D,), jnp.float32)
    embed = 1.2 * jax.random.normal(jax.random.fold_in(key, 13), (CLASSES, D), jnp.float32)
    col_scale = jnp.exp(jax.random.uniform(jax.random.fold_in(key, 14), (D,), jnp.float32, -1.1513, 1.1513))
    row_scale = jnp.exp(jax.random.uniform(jax.random.fold_in(key, 15), (TOKENS,), jnp.float32, -1.1513, 1.1513))
    drift = 1.0 + 2.0 * jnp.arange(TOKENS, dtype=jnp.float32) / (TOKENS - 1)
    mixing = jax.random.normal(jax.random.fold_in(key, 19), (latent_count, D), jnp.float32) / jnp.sqrt(jnp.float32(latent_count))
    signal = offset[None, :] + embed[classes]
    noise = jax.random.normal(jax.random.fold_in(key, 16), (TOKENS, D), jnp.float32)
    latent = jax.random.normal(jax.random.fold_in(key, 20), (TOKENS, latent_count), jnp.float32)
    linked = jnp.dot(latent, mixing, precision=lax.Precision.HIGHEST)
    values = drift[:, None] * signal + row_scale[:, None] * col_scale[None, :] * (noise + 2.0 * linked)
    return values.astype(jnp.bfloat16)


def setup_inputs(seed: int = 0) -> dict:
    key_list = jax.random.split(jax.random.key(seed), 3)
    return {
        "activations": draw_activations(jax.random.fold_in(key_list[2], 71), 0),
        "labels": draw_labels(jax.random.fold_in(key_list[2], 71), 0),
    }


def product(left, right):
    return lax.dot_general(left.astype(jnp.float32), right.astype(jnp.float32), (((0,), (0,)), ((), ())), precision=lax.Precision.HIGHEST, preferred_element_type=jnp.float32)


def reference(activations, labels):
    count = activations.shape[0]
    block = D // N_FEAT
    rows = activations.reshape(N_TOK, TOK_DEV, D)
    tags = labels.reshape(N_TOK, TOK_DEV)

    def add_sum(carry, piece):
        return carry + jnp.sum(piece.astype(jnp.float32), axis=0), None

    column_total, _ = lax.scan(add_sum, jnp.zeros((D,), jnp.float32), rows)
    mean = column_total / count
    classes = jnp.arange(CLASSES, dtype=jnp.int32)

    def add_terms(carry, item):
        piece, tag = item
        centered = (piece.astype(jnp.float32) - mean).astype(jnp.bfloat16)
        onehot = (tag[:, None] == classes[None, :]).astype(jnp.bfloat16)
        panel = centered.reshape(TOK_DEV, N_FEAT, block)[:, :, :PANEL].reshape(TOK_DEV, N_FEAT * PANEL)
        cov_acc = carry[0] + product(panel, centered)
        class_acc = carry[1] + product(onehot, centered)
        return (cov_acc, class_acc), None

    start = (jnp.zeros((N_FEAT * PANEL, D), jnp.float32), jnp.zeros((CLASSES, D), jnp.float32))
    sums, _ = lax.scan(add_terms, start, (rows, tags))
    cov_panel = sums[0] / (count - 1)
    cross_cov = sums[1] / count
    return cov_panel, cross_cov
```

```python
import functools

import jax
import jax.numpy as jnp
from jax import lax
from jax.experimental import pallas as pl
from jax.experimental.pallas import tpu as pltpu
from jax.sharding import PartitionSpec as P

CLASSES = 8
PANEL = 128
NZ, NYH, NX = 8, 2, 4
NY, NC = 4, 2
NF = NY * NC
Q = 4
ROWS = PANEL // Q
MESH = pl.DeviceIdType.MESH
F32 = jnp.float32
BF16 = jnp.bfloat16


def chunk_column(row):
    q0 = (row >> 5) & 1
    q1 = (row >> 6) & 1
    x = (row >> 3) & 3
    return 16 * (q0 * 4 + x) + 8 * q1 + (row & 7)


def to_tile(row_value, ref):
    for i in range(8):
        ref[i : i + 1, :] = row_value[:, 128 * i : 128 * (i + 1)]


def kernel(
    act_hbm, labels_ref, cov_ref, cross_ref,
    abuf, cbuf, pan, lhs, accf, xs, xr, zsum, zs, zr, ykeep, ysend, yr,
    mz, mx, my, mf, mrow, mcol, crs, crr, cx, cy, cg,
    load_sem, ag_r, ag_right, ag_left, ag_part,
    x_s, x_r, z_s, z_r, y_s, y_r,
    mz_s, mz_r, mx_s, mx_r, my_s, my_r, mf_s, mf_r,
    cr_s, cr_r, cx_s, cx_r, cy_s, cy_r, cg_s, cg_r,
):
    tokens, width = abuf.shape
    tok = lax.axis_index("tok")
    feat = lax.axis_index("feat")
    z = tok // (NYH * NX)
    yh = (tok // NX) % NYH
    x = tok % NX
    y = feat // NC
    c = feat % NC
    total = tokens * NZ * NYH * NX

    def dev(zz=None, hh=None, xx=None, ff=None):
        zz = z if zz is None else zz
        hh = yh if hh is None else hh
        xx = x if xx is None else xx
        ff = feat if ff is None else ff
        return {"tok": (zz * NYH + hh) * NX + xx, "feat": ff}

    def remote(src, dst, send, recv, device):
        return pltpu.make_async_remote_copy(
            src_ref=src, dst_ref=dst, send_sem=send, recv_sem=recv,
            device_id=device, device_id_type=MESH,
        )

    first = pltpu.make_async_copy(
        act_hbm.at[:, pl.ds(0, PANEL)], abuf.at[:, pl.ds(0, PANEL)], load_sem.at[0])
    rest = pltpu.make_async_copy(
        act_hbm.at[:, pl.ds(PANEL, width - PANEL)],
        abuf.at[:, pl.ds(PANEL, width - PANEL)], load_sem.at[1])
    first.start()
    rest.start()

    barrier = pltpu.get_barrier_semaphore()
    for d in range(1, NF):
        pl.semaphore_signal(barrier, inc=1, device_id=dev(ff=(feat + d) % NF), device_id_type=MESH)
    for d in range(1, NZ):
        pl.semaphore_signal(barrier, inc=1, device_id=dev(zz=(z + d) % NZ), device_id_type=MESH)
    for d in range(1, NX):
        pl.semaphore_signal(barrier, inc=1, device_id=dev(xx=(x + d) % NX), device_id_type=MESH)
    pl.semaphore_signal(barrier, inc=1, device_id=dev(hh=1 - yh), device_id_type=MESH)

    first.wait()
    rows = lax.broadcasted_iota(jnp.int32, (PANEL, PANEL), 0)
    lanes = lax.broadcasted_iota(jnp.int32, (PANEL, PANEL), 1)
    pick = lanes == chunk_column(rows)
    select = jnp.where(pick, 1.0, 0.0).astype(BF16)
    for i in range(4):
        part = tokens // 4
        turned = lax.dot_general(
            select, abuf[i * part : (i + 1) * part, :PANEL],
            (((1,), (1,)), ((), ())), preferred_element_type=F32).astype(BF16)
        for q in range(Q):
            pan[q, feat, :, i * part : (i + 1) * part] = turned[q * ROWS : (q + 1) * ROWS, :]

    rest.wait()

    def add_rows(i, carry):
        block = abuf[pl.ds(pl.multiple_of(i * 64, 64), 64), :].astype(F32)
        return carry + jnp.sum(block.reshape(8, 8, width), axis=0)

    sums = lax.fori_loop(0, tokens // 64, add_rows, jnp.zeros((8, width), F32))
    to_tile(jnp.sum(sums, axis=0, keepdims=True), mz.at[z])

    pl.semaphore_wait(barrier, (NF - 1) + (NZ - 1) + (NX - 1) + 1)

    def panel_copy(q, f, device, send):
        return remote(pan.at[q, f], pan.at[q, f], send.at[q, f], ag_r.at[q, f], device)

    def go_right(q, f):
        return panel_copy(q, f, dev(ff=(feat + NC) % NF), ag_right)

    def go_left(q, f):
        return panel_copy(q, f, dev(ff=(feat + NF - NC) % NF), ag_left)

    def go_part(q, f):
        return panel_copy(q, f, dev(ff=y * NC + 1 - c), ag_part)

    def ag_own(q):
        @pl.when(y < NY - 1)
        def _():
            go_right(q, feat).start()

        @pl.when(y > 0)
        def _():
            go_left(q, feat).start()

        go_part(q, feat).start()

    def ag_recv(q):
        for k in range(1, NY):
            @pl.when(y >= k)
            def _():
                f = feat - NC * k
                go_part(q, f).wait_recv()

                @pl.when(y < NY - 1)
                def _():
                    go_right(q, f).start()

                go_part(q, f).start()

            @pl.when(y + k < NY)
            def _():
                f = feat + NC * k
                go_part(q, f).wait_recv()

                @pl.when(y > 0)
                def _():
                    go_left(q, f).start()

                go_part(q, f).start()

        for yy in range(NY):
            go_part(q, yy * NC + 1 - c).wait_recv()

    def ag_drain():
        for q in range(Q):
            for yy in range(NY):
                f = yy * NC + c

                @pl.when((y < NY - 1) & (y >= yy))
                def _():
                    go_right(q, f).wait_send()

                @pl.when((y > 0) & (y <= yy))
                def _():
                    go_left(q, f).wait_send()

                go_part(q, f).wait_send()

    def z_copy(buf, src, dst, send, recv, d):
        to = (z + d) % NZ
        return remote(src, dst, send.at[to], recv.at[z], dev(zz=to))

    def exchange_start(buf, own, n, send, recv, where):
        for d in range(1, n):
            to = (own + d) % n
            remote(buf.at[own], buf.at[own], send.at[to], recv.at[own], where(to)).start()

    def exchange_wait(buf, own, n, send, recv, where):
        for d in range(1, n):
            to = (own + d) % n
            remote(buf.at[own], buf.at[own], send.at[to], recv.at[own], where(to)).wait_send()
            remote(buf.at[to], buf.at[to], send.at[to], recv.at[to], where(to)).wait_recv()

    def at_z(to):
        return dev(zz=to)

    def at_x(to):
        return dev(xx=to)

    def at_h(to):
        return dev(hh=to)

    def at_f(to):
        return dev(ff=to)

    def slot_sum(buf, n):
        value = buf[0]
        for i in range(1, n):
            value = value + buf[i]
        return value

    def compute(q):
        for f in range(NF):
            block = pan[q, f].astype(F32) - mcol[f, q * ROWS : (q + 1) * ROWS, 0:1]
            lhs[f * ROWS : (f + 1) * ROWS, :] = block.astype(BF16)

        def columns(n, carry):
            at = pl.ds(pl.multiple_of(n * 256, 256), 256)
            acc = jnp.dot(lhs[...], cbuf[:, at], preferred_element_type=F32)
            acc = acc.reshape(NF, NX, 8, 256)
            for xx in range(NX):
                slab = acc[:, xx].reshape(NF * 8, 256)
                accf[q, xx, :, at] = slab
                xs[q, xx, :, at] = slab.astype(BF16)
            return carry

        lax.fori_loop(0, width // 256, columns, 0)
        for d in range(1, NX):
            x_copy(q, d).start()

    def x_copy(q, d):
        to = (x + d) % NX
        return remote(xs.at[q, to], xr.at[q, d - 1], x_s.at[q, d - 1], x_r.at[q, d - 1], dev(xx=to))

    def z_send(q, d):
        to = (z + d) % NZ
        return remote(zs.at[q, to], zr.at[q, d - 1], z_s.at[q, d - 1], z_r.at[q, d - 1], dev(zz=to))

    def zphase(q):
        for d in range(1, NX):
            x_copy(q, d).wait_recv()
        for f in range(NF):
            at = slice(f * 8, f * 8 + 8)
            value = accf[q, x, at, :]
            for d in range(NX - 1):
                value = value + xr[q, d, at, :].astype(F32)
            zsum[q, f] = value
            half = width // 2
            zs[q, f] = jnp.concatenate([value[:, :half], value[:, half:]], axis=0).astype(BF16)
        for d in range(1, NZ):
            z_send(q, d).start()

    def y_send(half):
        return remote(ysend.at[half], yr.at[half], y_s.at[half], y_r.at[half], dev(hh=1 - yh))

    def yphase(q):
        for d in range(1, NZ):
            z_send(q, d).wait_recv()
        parts = jnp.zeros((16, width // 2), F32)
        for d in range(NZ - 1):
            parts = parts + zr[q, d].astype(F32)
        value = zsum[q, z] + jnp.concatenate([parts[:8], parts[8:]], axis=1)
        half = q // 2

        @pl.when(yh == q % 2)
        def _():
            ykeep[half] = value

        @pl.when(yh != q % 2)
        def _():
            ysend[half] = value
            y_send(half).start()

    exchange_start(mz, z, NZ, mz_s, mz_r, at_z)
    ag_own(0)
    ag_own(1)
    exchange_wait(mz, z, NZ, mz_s, mz_r, at_z)
    mx[x] = slot_sum(mz, NZ)
    exchange_start(mx, x, NX, mx_s, mx_r, at_x)
    ag_recv(0)
    exchange_wait(mx, x, NX, mx_s, mx_r, at_x)
    my[yh] = slot_sum(mx, NX)
    exchange_start(my, yh, NYH, my_s, my_r, at_h)
    ag_own(2)
    exchange_wait(my, yh, NYH, my_s, my_r, at_h)
    mean = slot_sum(my, NYH) / total
    mf[feat] = mean
    exchange_start(mf, feat, NF, mf_s, mf_r, at_f)
    for i in range(8):
        mrow[:, 128 * i : 128 * (i + 1)] = mean[i : i + 1, :]

    def center(i, carry):
        at = pl.ds(pl.multiple_of(i * 64, 64), 64)
        cbuf[at, :] = (abuf[at, :].astype(F32) - mrow[...]).astype(BF16)
        return carry

    lax.fori_loop(0, tokens // 64, center, 0)
    ag_recv(1)
    ag_own(3)

    exchange_wait(mf, feat, NF, mf_s, mf_r, at_f)
    for f in range(NF):
        value = jnp.where(pick, mf[f, 0:1, :], 0.0)
        mcol[f] = jnp.broadcast_to(jnp.sum(value, axis=1, keepdims=True), (PANEL, PANEL))

    compute(0)
    compute(1)

    classes = lax.broadcasted_iota(jnp.int32, (16, tokens), 0)
    onehot = jnp.where(classes == labels_ref[...], 1.0, 0.0).astype(BF16)

    def class_columns(n, carry):
        at = pl.ds(pl.multiple_of(n * 256, 256), 256)
        part = jnp.dot(onehot, cbuf[:, at], preferred_element_type=F32)
        for k in range(CLASSES):
            for i in range(2):
                crs[k, pl.ds(2 * n + i, 1), :] = part[k : k + 1, 128 * i : 128 * (i + 1)]
        return carry

    lax.fori_loop(0, width // 256, class_columns, 0)
    crr[z] = crs[z]

    def class_copy(d):
        to = (z + d) % NZ
        return remote(crs.at[to], crr.at[z], cr_s.at[to], cr_r.at[z], at_z(to))

    def class_from(d):
        to = (z + d) % NZ
        return remote(crs.at[to], crr.at[to], cr_s.at[to], cr_r.at[to], at_z(to))

    for d in range(1, NZ):
        class_copy(d).start()

    zphase(0)
    ag_recv(2)
    compute(2)

    for d in range(1, NZ):
        class_copy(d).wait_send()
        class_from(d).wait_recv()
    cx[x] = slot_sum(crr, NZ)
    exchange_start(cx, x, NX, cx_s, cx_r, at_x)

    zphase(1)
    yphase(0)

    exchange_wait(cx, x, NX, cx_s, cx_r, at_x)
    cy[yh] = slot_sum(cx, NX)
    exchange_start(cy, yh, NYH, cy_s, cy_r, at_h)

    ag_recv(3)
    compute(3)

    exchange_wait(cy, yh, NYH, cy_s, cy_r, at_h)
    cg[z] = slot_sum(cy, NYH)
    exchange_start(cg, z, NZ, cg_s, cg_r, at_z)

    zphase(2)
    yphase(1)
    zphase(3)

    exchange_wait(cg, z, NZ, cg_s, cg_r, at_z)
    for k in range(CLASSES):
        for i in range(8):
            cross_ref[k : k + 1, 128 * i : 128 * (i + 1)] = cg[k, i : i + 1, :] / total

    yphase(2)
    yphase(3)
    for half in range(2):
        y_send(half).wait_recv()
        cov_ref[8 * half : 8 * half + 8, :] = (ykeep[half] + yr[half]) / (total - 1)

    ag_drain()
    for q in range(Q):
        for d in range(1, NX):
            x_copy(q, d).wait_send()
        for d in range(1, NZ):
            z_send(q, d).wait_send()
    for half in range(2):
        y_send(half).wait_send()


def body(activations, labels):
    tokens, width = activations.shape
    dma = pltpu.SemaphoreType.DMA
    vm = pltpu.VMEM
    tile = (8, 128)
    scratch = [
        vm((tokens, width), BF16),
        vm((tokens, width), BF16),
        vm((Q, NF, ROWS, tokens), BF16),
        vm((NF * ROWS, tokens), BF16),
        vm((Q, NX, NF * 8, width), F32),
        vm((Q, NX, NF * 8, width), BF16),
        vm((Q, NX - 1, NF * 8, width), BF16),
        vm((Q, NF, 8, width), F32),
        vm((Q, NZ, 16, width // 2), BF16),
        vm((Q, NZ - 1, 16, width // 2), BF16),
        vm((2, 8, width), F32),
        vm((2, 8, width), F32),
        vm((2, 8, width), F32),
        vm((NZ, *tile), F32),
        vm((NX, *tile), F32),
        vm((NYH, *tile), F32),
        vm((NF, *tile), F32),
        vm((1, width), F32),
        vm((NF, PANEL, PANEL), F32),
        vm((CLASSES, *tile), F32),
        vm((NZ, *tile), F32),
        vm((NX, *tile), F32),
        vm((NYH, *tile), F32),
        vm((NZ, *tile), F32),
        dma((2,)),
        dma((Q, NF)), dma((Q, NF)), dma((Q, NF)), dma((Q, NF)),
        dma((Q, NX - 1)), dma((Q, NX - 1)),
        dma((Q, NZ - 1)), dma((Q, NZ - 1)),
        dma((2,)), dma((2,)),
        dma((NZ,)), dma((NZ,)), dma((NX,)), dma((NX,)), dma((NYH,)), dma((NYH,)),
        dma((NF,)), dma((NF,)),
        dma((NZ,)), dma((NZ,)), dma((NX,)), dma((NX,)), dma((NYH,)), dma((NYH,)),
        dma((NZ,)), dma((NZ,)),
    ]
    out_rows = NF * PANEL // (NZ * NYH * NX)
    return pl.pallas_call(
        kernel,
        out_shape=(
            jax.ShapeDtypeStruct((out_rows, width), F32),
            jax.ShapeDtypeStruct((CLASSES, width), F32),
        ),
        in_specs=[
            pl.BlockSpec(memory_space=pl.ANY),
            pl.BlockSpec(memory_space=pltpu.VMEM),
        ],
        out_specs=(
            pl.BlockSpec(memory_space=pltpu.VMEM),
            pl.BlockSpec(memory_space=pltpu.VMEM),
        ),
        scratch_shapes=scratch,
        compiler_params=pltpu.CompilerParams(
            collective_id=0, has_side_effects=True, vmem_limit_bytes=48 * 2**20
        ),
        name="stats",
    )(activations, labels.reshape(1, tokens))


def solution(mesh):
    in_specs = (P("tok", "feat"), P("tok"))
    out_specs = (P("tok", "feat"), P(None, "feat"))
    return jax.shard_map(body, mesh=mesh, in_specs=in_specs, out_specs=out_specs, check_vma=False)
```

```python
import functools

import jax
import jax.numpy as jnp
from jax import lax
from jax.experimental import pallas as pl
from jax.experimental.pallas import tpu as pltpu
from jax.sharding import PartitionSpec as P

CLASSES = 8
PANEL = 128
NZ, NYH, NX = 8, 2, 4
NY, NC = 4, 2
NF = NY * NC
Q = 8
ROWS = PANEL // Q
MESH = pl.DeviceIdType.MESH
F32 = jnp.float32
BF16 = jnp.bfloat16


def chunk_column(row):
    quarter = row >> 5
    place = (row >> 2) & 7
    return 16 * place + 4 * quarter + (row & 3)


def fold(even, odd):
    low = lax.broadcasted_iota(jnp.int32, even.shape, 0) < 4
    return jnp.where(low, even, pltpu.roll(odd, 4, 0))


def fold_upper(even, odd):
    low = lax.broadcasted_iota(jnp.int32, even.shape, 0) < 4
    return jnp.where(low, pltpu.roll(even, 4, 0), odd)


def to_tile(row_value, ref):
    for i in range(8):
        ref[i : i + 1, :] = row_value[:, 128 * i : 128 * (i + 1)]


def kernel(
    act_hbm, labels_hbm, cov_ref, cross_ref,
    abuf, labels_ref, cbuf, pan, lhs, accf, xs, xr, zsum, zs, zr, ykeep, ysend, yr,
    mz, mx, my, mf, mrow, mcol, crs, crr, cx, cy, cg,
    load_sem, ag_r, ag_right, ag_left, ag_part,
    x_s, x_r, z_s, z_r, y_s, y_r,
    mz_s, mz_r, mx_s, mx_r, my_s, my_r, mf_s, mf_r,
    cr_s, cr_r, cx_s, cx_r, cy_s, cy_r, cg_s, cg_r,
):
    tokens, width = abuf.shape
    tok = lax.axis_index("tok")
    feat = lax.axis_index("feat")
    z = tok // (NYH * NX)
    yh = (tok // NX) % NYH
    x = tok % NX
    y = feat // NC
    c = feat % NC
    total = tokens * NZ * NYH * NX

    def dev(zz=None, hh=None, xx=None, ff=None):
        zz = z if zz is None else zz
        hh = yh if hh is None else hh
        xx = x if xx is None else xx
        ff = feat if ff is None else ff
        return {"tok": (zz * NYH + hh) * NX + xx, "feat": ff}

    def remote(src, dst, send, recv, device):
        return pltpu.make_async_remote_copy(
            src_ref=src, dst_ref=dst, send_sem=send, recv_sem=recv,
            device_id=device, device_id_type=MESH,
        )

    first = pltpu.make_async_copy(
        act_hbm.at[:, pl.ds(0, PANEL)], abuf.at[:, pl.ds(0, PANEL)], load_sem.at[0])
    rest = pltpu.make_async_copy(
        act_hbm.at[:, pl.ds(PANEL, width - PANEL)],
        abuf.at[:, pl.ds(PANEL, width - PANEL)], load_sem.at[1])
    tags = pltpu.make_async_copy(labels_hbm, labels_ref, load_sem.at[2])
    first.start()
    rest.start()
    tags.start()

    barrier = pltpu.get_barrier_semaphore()
    for d in range(1, NF):
        pl.semaphore_signal(barrier, inc=1, device_id=dev(ff=(feat + d) % NF), device_id_type=MESH)
    for d in range(1, NZ):
        pl.semaphore_signal(barrier, inc=1, device_id=dev(zz=(z + d) % NZ), device_id_type=MESH)
    for d in range(1, NX):
        pl.semaphore_signal(barrier, inc=1, device_id=dev(xx=(x + d) % NX), device_id_type=MESH)
    pl.semaphore_signal(barrier, inc=1, device_id=dev(hh=1 - yh), device_id_type=MESH)

    first.wait()
    rows = lax.broadcasted_iota(jnp.int32, (PANEL, PANEL), 0)
    lanes = lax.broadcasted_iota(jnp.int32, (PANEL, PANEL), 1)
    pick = lanes == chunk_column(rows)
    select = jnp.where(pick, 1.0, 0.0).astype(BF16)
    for i in range(4):
        part = tokens // 4
        turned = lax.dot_general(
            select, abuf[i * part : (i + 1) * part, :PANEL],
            (((1,), (1,)), ((), ())), preferred_element_type=F32).astype(BF16)
        for q in range(Q):
            pan[q, feat, :, i * part : (i + 1) * part] = turned[q * ROWS : (q + 1) * ROWS, :]

    pl.semaphore_wait(barrier, (NF - 1) + (NZ - 1) + (NX - 1) + 1)

    def panel_copy(q, f, device, send):
        return remote(pan.at[q, f], pan.at[q, f], send.at[q, f], ag_r.at[q, f], device)

    def go_right(q, f):
        return panel_copy(q, f, dev(ff=(feat + NC) % NF), ag_right)

    def go_left(q, f):
        return panel_copy(q, f, dev(ff=(feat + NF - NC) % NF), ag_left)

    def go_part(q, f):
        return panel_copy(q, f, dev(ff=y * NC + 1 - c), ag_part)

    def ag_own(q):
        @pl.when(y < NY - 1)
        def _():
            go_right(q, feat).start()

        @pl.when(y > 0)
        def _():
            go_left(q, feat).start()

        go_part(q, feat).start()

    def ag_recv_step(q, k):
        @pl.when(y >= k)
        def _():
            f = feat - NC * k
            go_part(q, f).wait_recv()

            @pl.when(y < NY - 1)
            def _():
                go_right(q, f).start()

            go_part(q, f).start()

        @pl.when(y + k < NY)
        def _():
            f = feat + NC * k
            go_part(q, f).wait_recv()

            @pl.when(y > 0)
            def _():
                go_left(q, f).start()

            go_part(q, f).start()

    def ag_recv(q, first_step=1):
        for k in range(first_step, NY):
            ag_recv_step(q, k)

    def ag_recv_part(q):
        for yy in range(NY):
            go_part(q, yy * NC + 1 - c).wait_recv()

    def ag_drain():
        for q in range(Q):
            for yy in range(NY):
                f = yy * NC + c

                @pl.when((y < NY - 1) & (y >= yy))
                def _():
                    go_right(q, f).wait_send()

                @pl.when((y > 0) & (y <= yy))
                def _():
                    go_left(q, f).wait_send()

                go_part(q, f).wait_send()

    def z_copy(buf, src, dst, send, recv, d):
        to = (z + d) % NZ
        return remote(src, dst, send.at[to], recv.at[z], dev(zz=to))

    def exchange_start(buf, own, n, send, recv, where):
        for d in range(1, n):
            to = (own + d) % n
            remote(buf.at[own], buf.at[own], send.at[to], recv.at[own], where(to)).start()

    def exchange_wait(buf, own, n, send, recv, where):
        for d in range(1, n):
            to = (own + d) % n
            remote(buf.at[own], buf.at[own], send.at[to], recv.at[own], where(to)).wait_send()
            remote(buf.at[to], buf.at[to], send.at[to], recv.at[to], where(to)).wait_recv()

    def at_z(to):
        return dev(zz=to)

    def at_x(to):
        return dev(xx=to)

    def at_h(to):
        return dev(hh=to)

    def at_f(to):
        return dev(ff=to)

    def slot_sum(buf, n):
        value = buf[0]
        for i in range(1, n):
            value = value + buf[i]
        return value

    half = width // 2
    quarter = width // 4
    side_a, side_b = pl.ds(0, half), pl.ds(half, half)

    def compute(q):
        ag_recv_part(q)
        for f in range(NF):
            block = pan[q, f].astype(F32) - mcol[f, q * ROWS : (q + 1) * ROWS, 0:1]
            lhs[f * ROWS : (f + 1) * ROWS, :] = block.astype(BF16)

        def columns(n, carry):
            at = pl.ds(pl.multiple_of(n * 256, 256), 256)
            acc = jnp.dot(lhs[...], cbuf[:, at], preferred_element_type=F32)
            acc = acc.reshape(NF // 2, 2, NX // 2, 8, 256)
            for xx in range(NX):
                join = fold_upper if xx % 2 else fold
                rows = [join(acc[i, 0, xx // 2], acc[i, 1, xx // 2]) for i in range(NF // 2)]
                slab = jnp.concatenate(rows, axis=0)
                accf[q, xx, :, at] = slab
                xs[q, xx, :, at] = slab.astype(BF16)
            return carry

        lax.fori_loop(0, width // 256, columns, 0)
        for m in range(4):
            x_copy(q, m).start()

    right, left, across = (x + 1) % NX, (x + NX - 1) % NX, (x + 2) % NX

    def x_copy(q, m):
        slab = (across, across, right, left, right, left)[m]
        side = (side_a, side_b, side_b, side_a, side_a, side_b)[m]
        to = (right, left)[m % 2]
        return remote(xs.at[q, slab, :, side], xr.at[q, m], x_s.at[q, m], x_r.at[q, m], dev(xx=to))

    def xphase(q):
        for m, slab, side in ((4, right, side_a), (5, left, side_b)):
            x_copy(q, m - 4).wait_recv()
            xs[q, slab, :, side] = (accf[q, slab, :, side] + xr[q, m - 4].astype(F32)).astype(BF16)
            x_copy(q, m).start()

    def z_send(q, d):
        to = (z + d) % NZ
        return remote(zs.at[q, to], zr.at[q, d - 1], z_s.at[q, d - 1], z_r.at[q, d - 1], dev(zz=to))

    def zphase(q):
        for m in range(2, 6):
            x_copy(q, m).wait_recv()
        value_a = accf[q, x, :, side_a] + xr[q, 4].astype(F32) + xr[q, 3].astype(F32)
        value_b = accf[q, x, :, side_b] + xr[q, 2].astype(F32) + xr[q, 5].astype(F32)
        for f in range(NF):
            join = fold_upper if f % 2 else fold
            at = slice(f // 2 * 8, f // 2 * 8 + 8)
            packed = jnp.concatenate(
                [join(v[at, :quarter], v[at, quarter:]) for v in (value_a, value_b)], axis=0)
            zsum[q, f] = packed
            zs[q, f] = packed.astype(BF16)
        for d in range(1, NZ):
            z_send(q, d).start()

    def y_send(n):
        return remote(ysend.at[n], yr.at[n], y_s.at[n], y_r.at[n], dev(hh=1 - yh))

    def yphase(q):
        for d in range(1, NZ):
            z_send(q, d).wait_recv()
        value = zsum[q, z]
        for d in range(NZ - 1):
            value = value + zr[q, d].astype(F32)
        n = q // 2

        @pl.when(yh == q % 2)
        def _():
            ykeep[n] = value

        @pl.when(yh != q % 2)
        def _():
            ysend[n] = value
            y_send(n).start()

    for q in range(4):
        ag_own(q)
    rest.wait()

    def add_rows(i, carry):
        block = abuf[pl.ds(pl.multiple_of(i * 64, 64), 64), :].astype(F32)
        return carry + jnp.sum(block.reshape(8, 8, width), axis=0)

    sums = lax.fori_loop(0, tokens // 64, add_rows, jnp.zeros((8, width), F32))
    to_tile(jnp.sum(sums, axis=0, keepdims=True), mz.at[z])


    exchange_start(mz, z, NZ, mz_s, mz_r, at_z)
    ag_recv_step(0, 1)
    exchange_wait(mz, z, NZ, mz_s, mz_r, at_z)
    mx[x] = slot_sum(mz, NZ)
    exchange_start(mx, x, NX, mx_s, mx_r, at_x)
    ag_recv(0, 2)
    ag_own(4)
    exchange_wait(mx, x, NX, mx_s, mx_r, at_x)
    my[yh] = slot_sum(mx, NX)
    exchange_start(my, yh, NYH, my_s, my_r, at_h)
    ag_recv(1)
    ag_own(5)
    exchange_wait(my, yh, NYH, my_s, my_r, at_h)
    mean = slot_sum(my, NYH) / total
    mf[feat] = mean
    exchange_start(mf, feat, NF, mf_s, mf_r, at_f)
    for i in range(8):
        mrow[:, 128 * i : 128 * (i + 1)] = mean[i : i + 1, :]

    def center(i, carry):
        at = pl.ds(pl.multiple_of(i * 64, 64), 64)
        cbuf[at, :] = (abuf[at, :].astype(F32) - mrow[...]).astype(BF16)
        return carry

    lax.fori_loop(0, tokens // 64, center, 0)
    ag_recv(2)
    ag_own(6)

    exchange_wait(mf, feat, NF, mf_s, mf_r, at_f)
    for f in range(NF):
        value = jnp.where(pick, mf[f, 0:1, :], 0.0)
        mcol[f] = jnp.broadcast_to(jnp.sum(value, axis=1, keepdims=True), (PANEL, PANEL))

    ag_recv(3)
    ag_own(7)
    compute(0)
    compute(1)
    ag_recv(4)
    compute(2)

    tags.wait()
    classes = lax.broadcasted_iota(jnp.int32, (16, tokens), 0)
    onehot = jnp.where(classes == labels_ref[...], 1.0, 0.0).astype(BF16)

    def class_columns(n, carry):
        at = pl.ds(pl.multiple_of(n * 256, 256), 256)
        part = jnp.dot(onehot, cbuf[:, at], preferred_element_type=F32)
        for k in range(CLASSES):
            for i in range(2):
                crs[k, pl.ds(2 * n + i, 1), :] = part[k : k + 1, 128 * i : 128 * (i + 1)]
        return carry

    lax.fori_loop(0, width // 256, class_columns, 0)
    crr[z] = crs[z]

    def class_copy(d):
        to = (z + d) % NZ
        return remote(crs.at[to], crr.at[z], cr_s.at[to], cr_r.at[z], at_z(to))

    def class_from(d):
        to = (z + d) % NZ
        return remote(crs.at[to], crr.at[to], cr_s.at[to], cr_r.at[to], at_z(to))

    for d in range(1, NZ):
        class_copy(d).start()

    xphase(0)
    xphase(1)
    compute(3)
    ag_recv(5)
    zphase(0)
    xphase(2)
    compute(4)

    for d in range(1, NZ):
        class_copy(d).wait_send()
        class_from(d).wait_recv()
    cx[x] = slot_sum(crr, NZ)
    exchange_start(cx, x, NX, cx_s, cx_r, at_x)

    zphase(1)
    xphase(3)
    ag_recv(6)
    compute(5)
    zphase(2)
    xphase(4)

    exchange_wait(cx, x, NX, cx_s, cx_r, at_x)
    cy[yh] = slot_sum(cx, NX)
    exchange_start(cy, yh, NYH, cy_s, cy_r, at_h)

    ag_recv(7)
    compute(6)
    zphase(3)
    xphase(5)
    compute(7)

    zphase(4)
    xphase(6)
    exchange_wait(cy, yh, NYH, cy_s, cy_r, at_h)
    cg[z] = slot_sum(cy, NYH)
    exchange_start(cg, z, NZ, cg_s, cg_r, at_z)
    zphase(5)
    xphase(7)
    zphase(6)
    yphase(0)
    yphase(1)
    yphase(2)
    zphase(7)
    yphase(3)
    yphase(4)
    yphase(5)
    yphase(6)

    exchange_wait(cg, z, NZ, cg_s, cg_r, at_z)
    for k in range(CLASSES):
        for i in range(8):
            cross_ref[k : k + 1, 128 * i : 128 * (i + 1)] = cg[k, i : i + 1, :] / total

    yphase(7)
    for n in range(Q // 2):
        y_send(n).wait_recv()
        value = (ykeep[n] + yr[n]) / (total - 1)
        for i in range(4):
            cov_ref[4 * n : 4 * n + 4, quarter * i : quarter * (i + 1)] = value[4 * i : 4 * i + 4, :]

    ag_drain()
    for q in range(Q):
        for m in range(6):
            x_copy(q, m).wait_send()
        for d in range(1, NZ):
            z_send(q, d).wait_send()
    for n in range(Q // 2):
        y_send(n).wait_send()


def body(activations, labels):
    tokens, width = activations.shape
    dma = pltpu.SemaphoreType.DMA
    vm = pltpu.VMEM
    tile = (8, 128)
    scratch = [
        vm((tokens, width), BF16),
        vm((1, tokens), jnp.int32),
        vm((tokens, width), BF16),
        vm((Q, NF, ROWS, tokens), BF16),
        vm((NF * ROWS, tokens), BF16),
        vm((Q, NX, NF * 4, width), F32),
        vm((Q, NX, NF * 4, width), BF16),
        vm((Q, 6, NF * 4, width // 2), BF16),
        vm((Q, NF, 16, width // 4), F32),
        vm((Q, NZ, 16, width // 4), BF16),
        vm((Q, NZ - 1, 16, width // 4), BF16),
        vm((Q // 2, 16, width // 4), F32),
        vm((Q // 2, 16, width // 4), F32),
        vm((Q // 2, 16, width // 4), F32),
        vm((NZ, *tile), F32),
        vm((NX, *tile), F32),
        vm((NYH, *tile), F32),
        vm((NF, *tile), F32),
        vm((1, width), F32),
        vm((NF, PANEL, PANEL), F32),
        vm((CLASSES, *tile), F32),
        vm((NZ, *tile), F32),
        vm((NX, *tile), F32),
        vm((NYH, *tile), F32),
        vm((NZ, *tile), F32),
        dma((3,)),
        dma((Q, NF)), dma((Q, NF)), dma((Q, NF)), dma((Q, NF)),
        dma((Q, 6)), dma((Q, 6)),
        dma((Q, NZ - 1)), dma((Q, NZ - 1)),
        dma((Q // 2,)), dma((Q // 2,)),
        dma((NZ,)), dma((NZ,)), dma((NX,)), dma((NX,)), dma((NYH,)), dma((NYH,)),
        dma((NF,)), dma((NF,)),
        dma((NZ,)), dma((NZ,)), dma((NX,)), dma((NX,)), dma((NYH,)), dma((NYH,)),
        dma((NZ,)), dma((NZ,)),
    ]
    out_rows = NF * PANEL // (NZ * NYH * NX)
    return pl.pallas_call(
        kernel,
        out_shape=(
            jax.ShapeDtypeStruct((out_rows, width), F32),
            jax.ShapeDtypeStruct((CLASSES, width), F32),
        ),
        in_specs=[
            pl.BlockSpec(memory_space=pl.ANY),
            pl.BlockSpec(memory_space=pl.ANY),
        ],
        out_specs=(
            pl.BlockSpec(memory_space=pltpu.VMEM),
            pl.BlockSpec(memory_space=pltpu.VMEM),
        ),
        scratch_shapes=scratch,
        compiler_params=pltpu.CompilerParams(
            collective_id=0, has_side_effects=True, vmem_limit_bytes=60 * 2**20
        ),
        name="stats",
    )(activations, labels.reshape(1, tokens))


def solution(mesh):
    in_specs = (P("tok", "feat"), P("tok"))
    out_specs = (P("tok", "feat"), P(None, "feat"))
    return jax.shard_map(body, mesh=mesh, in_specs=in_specs, out_specs=out_specs, check_vma=False)
```

```python
import functools

import jax
import jax.numpy as jnp
from jax import lax
from jax.experimental import pallas as pl
from jax.experimental.pallas import tpu as pltpu
from jax.sharding import PartitionSpec as P

CLASSES = 8
PANEL = 128
NZ, NYH, NX = 8, 2, 4
NY, NC = 4, 2
NF = NY * NC
Q = 8
ROWS = PANEL // Q
MESH = pl.DeviceIdType.MESH
F32 = jnp.float32
BF16 = jnp.bfloat16


def chunk_column(row):
    quarter = row >> 5
    place = (row >> 2) & 7
    return 16 * place + 4 * quarter + (row & 3)


def fold(even, odd):
    low = lax.broadcasted_iota(jnp.int32, even.shape, 0) < 4
    return jnp.where(low, even, pltpu.roll(odd, 4, 0))


def fold_upper(even, odd):
    low = lax.broadcasted_iota(jnp.int32, even.shape, 0) < 4
    return jnp.where(low, pltpu.roll(even, 4, 0), odd)


def to_tile(row_value, ref):
    for i in range(8):
        ref[i : i + 1, :] = row_value[:, 128 * i : 128 * (i + 1)]


def kernel(
    act_hbm, labels_hbm, cov_ref, cross_ref,
    abuf, labels_ref, cbuf, pan, lhs, accf, xs, xr, zsum, zs, zr, ykeep, ysend, yr,
    mz, mx, my, mf, mrow, mcol, crs, crr, cx, cy, cg,
    load_sem, ag_r, ag_pr, ag_s, x_s, x_r, z_s, z_r, y_s, y_r,
    mz_s, mz_r, mx_s, mx_r, my_s, my_r, mf_s, mf_r,
    cr_s, cr_r, cx_s, cx_r, cy_s, cy_r, cg_s, cg_r,
):
    tokens, width = abuf.shape
    tok = lax.axis_index("tok")
    feat = lax.axis_index("feat")
    z = tok // (NYH * NX)
    yh = (tok // NX) % NYH
    x = tok % NX
    y = feat // NC
    c = feat % NC
    total = tokens * NZ * NYH * NX

    def dev(zz=None, hh=None, xx=None, ff=None):
        zz = z if zz is None else zz
        hh = yh if hh is None else hh
        xx = x if xx is None else xx
        ff = feat if ff is None else ff
        return {"tok": (zz * NYH + hh) * NX + xx, "feat": ff}

    def remote(src, dst, send, recv, device):
        return pltpu.make_async_remote_copy(
            src_ref=src, dst_ref=dst, send_sem=send, recv_sem=recv,
            device_id=device, device_id_type=MESH,
        )

    first = pltpu.make_async_copy(
        act_hbm.at[:, pl.ds(0, PANEL)], abuf.at[:, pl.ds(0, PANEL)], load_sem.at[0])
    rest = pltpu.make_async_copy(
        act_hbm.at[:, pl.ds(PANEL, width - PANEL)],
        abuf.at[:, pl.ds(PANEL, width - PANEL)], load_sem.at[1])
    tags = pltpu.make_async_copy(labels_hbm, labels_ref, load_sem.at[2])
    first.start()
    rest.start()
    tags.start()

    barrier = pltpu.get_barrier_semaphore()
    for d in range(1, NF):
        pl.semaphore_signal(barrier, inc=1, device_id=dev(ff=(feat + d) % NF), device_id_type=MESH)
    for d in range(1, NZ):
        pl.semaphore_signal(barrier, inc=1, device_id=dev(zz=(z + d) % NZ), device_id_type=MESH)
    for d in range(1, NX):
        pl.semaphore_signal(barrier, inc=1, device_id=dev(xx=(x + d) % NX), device_id_type=MESH)
    pl.semaphore_signal(barrier, inc=1, device_id=dev(hh=1 - yh), device_id_type=MESH)

    first.wait()
    rows = lax.broadcasted_iota(jnp.int32, (PANEL, PANEL), 0)
    lanes = lax.broadcasted_iota(jnp.int32, (PANEL, PANEL), 1)
    pick = lanes == chunk_column(rows)
    select = jnp.where(pick, 1.0, 0.0).astype(BF16)
    for i in range(4):
        part = tokens // 4
        turned = lax.dot_general(
            select, abuf[i * part : (i + 1) * part, :PANEL],
            (((1,), (1,)), ((), ())), preferred_element_type=F32).astype(BF16)
        for q in range(Q):
            pan[q, c, y, :, i * part : (i + 1) * part] = turned[q * ROWS : (q + 1) * ROWS, :]

    pl.semaphore_wait(barrier, (NF - 1) + (NZ - 1) + (NX - 1) + 1)

    def panel_copy(q, yy, to, n):
        to = jnp.clip(to, 0, NY - 1)
        return remote(
            pan.at[q, c, yy], pan.at[q, c, yy], ag_s.at[n], ag_r.at[q, yy], dev(ff=to * NC + c))

    def share_copy(q, yy):
        return remote(pan.at[q, c, yy], pan.at[q, c, yy], ag_s.at[5], ag_pr.at[q], dev(ff=y * NC + 1 - c))

    def ag_own(q):
        for n, step in enumerate((1, -1, 2, -2)):
            @pl.when((y + step >= 0) & (y + step < NY))
            def _():
                panel_copy(q, y, y + step, n).start()

        share_copy(q, y).start()

    def got(q, yy):
        panel_copy(q, yy, y, 0).wait_recv()
        share_copy(q, yy).start()

    def forward(q):
        @pl.when(y == 2)
        def _():
            got(q, 0)
            panel_copy(q, 0, 3, 4).start()

        @pl.when(y == 1)
        def _():
            got(q, 3)
            panel_copy(q, 3, 0, 4).start()

    def share(q):
        for step in (1, -1, 2, -2, 3, -3):
            inside = (y + step >= 0) & (y + step < NY)
            if abs(step) == 2:
                inside = inside & ((y == 0) | (y == NY - 1))

            @pl.when(inside)
            def _():
                got(q, y + step)

    def ag_recv_part(q):
        remote(pan.at[q, 1 - c], pan.at[q, 1 - c], ag_s.at[5], ag_pr.at[q], dev(ff=y * NC + 1 - c)).wait_recv()

    def ag_drain():
        own = pan.at[:, c, y]
        for n, step in enumerate((1, -1, 2, -2)):
            @pl.when((y + step >= 0) & (y + step < NY))
            def _():
                remote(own, own, ag_s.at[n], ag_r.at[0, 0], dev(ff=y * NC + 1 - c)).wait_send()

        @pl.when((y == 1) | (y == 2))
        def _():
            remote(own, own, ag_s.at[4], ag_r.at[0, 0], dev(ff=y * NC + 1 - c)).wait_send()

        shared = pan.at[:, c]
        remote(shared, shared, ag_s.at[5], ag_r.at[0, 0], dev(ff=y * NC + 1 - c)).wait_send()

    def far_first(n):
        return sorted(range(1, n), key=lambda d: -min(d, n - d))

    def exchange_start(buf, own, n, send, recv, where):
        for d in far_first(n):
            to = (own + d) % n
            remote(buf.at[own], buf.at[own], send, recv, where(to)).start()

    def exchange_wait(buf, own, n, send, recv, where):
        rest_of = buf.at[pl.ds(0, n - 1)]
        every = remote(rest_of, rest_of, send, recv, where((own + 1) % n))
        every.wait_send()
        every.wait_recv()

    def at_z(to):
        return dev(zz=to)

    def at_x(to):
        return dev(xx=to)

    def at_h(to):
        return dev(hh=to)

    def at_f(to):
        return dev(ff=to)

    def slot_sum(buf, n):
        value = buf[0]
        for i in range(1, n):
            value = value + buf[i]
        return value

    half = width // 2
    quarter = width // 4
    side_a, side_b = pl.ds(0, half), pl.ds(half, half)

    def compute(q):
        ag_recv_part(q)
        for f in range(NF):
            block = pan[q, f % NC, f // NC].astype(F32) - mcol[f, q * ROWS : (q + 1) * ROWS, 0:1]
            lhs[f * ROWS : (f + 1) * ROWS, :] = block.astype(BF16)

        def columns(n, carry):
            at = pl.ds(pl.multiple_of(n * 256, 256), 256)
            acc = jnp.dot(lhs[...], cbuf[:, at], preferred_element_type=F32)
            acc = acc.reshape(NF // 2, 2, NX // 2, 8, 256)
            for xx in range(NX):
                join = fold_upper if xx % 2 else fold
                rows = [join(acc[i, 0, xx // 2], acc[i, 1, xx // 2]) for i in range(NF // 2)]
                slab = jnp.concatenate(rows, axis=0)
                accf[q, xx, :, at] = slab
                xs[q, xx, :, at] = slab.astype(BF16)
            return carry

        lax.fori_loop(0, width // 256, columns, 0)
        for m in range(4):
            x_copy(q, m).start()

    right, left, across = (x + 1) % NX, (x + NX - 1) % NX, (x + 2) % NX

    def x_copy(q, m):
        slab = (across, across, right, left, right, left)[m]
        side = (side_a, side_b, side_b, side_a, side_a, side_b)[m]
        to = (right, left)[m % 2]
        return remote(xs.at[q, slab, :, side], xr.at[q, m], x_s.at[m], x_r.at[q, min(m, 2)], dev(xx=to))

    def xphase(q):
        for m, slab, side in ((4, right, side_a), (5, left, side_b)):
            x_copy(q, m - 4).wait_recv()
            xs[q, slab, :, side] = (accf[q, slab, :, side] + xr[q, m - 4].astype(F32)).astype(BF16)
            x_copy(q, m).start()

    def z_send(q, d):
        to = (z + d) % NZ
        return remote(zs.at[q, to], zr.at[q, d - 1], z_s, z_r.at[q], dev(zz=to))

    def zphase(q):
        last = xr.at[q, 2:6]
        remote(last, last, x_s.at[2], x_r.at[q, 2], dev(xx=right)).wait_recv()
        value_a = accf[q, x, :, side_a] + xr[q, 4].astype(F32) + xr[q, 3].astype(F32)
        value_b = accf[q, x, :, side_b] + xr[q, 2].astype(F32) + xr[q, 5].astype(F32)
        for f in range(NF):
            join = fold_upper if f % 2 else fold
            at = slice(f // 2 * 8, f // 2 * 8 + 8)
            packed = jnp.concatenate(
                [join(v[at, :quarter], v[at, quarter:]) for v in (value_a, value_b)], axis=0)
            zsum[q, f] = packed
            zs[q, f] = packed.astype(BF16)
        for d in far_first(NZ):
            z_send(q, d).start()

    def y_send(n):
        return remote(ysend.at[n], yr.at[n], y_s, y_r, dev(hh=1 - yh))

    def yphase(q):
        remote(zr.at[q], zr.at[q], z_s, z_r.at[q], dev(zz=(z + 1) % NZ)).wait_recv()
        value = zsum[q, z]
        for d in range(NZ - 1):
            value = value + zr[q, d].astype(F32)
        n = q // 2

        @pl.when(yh == q % 2)
        def _():
            ykeep[n] = value

        @pl.when(yh != q % 2)
        def _():
            ysend[n] = value
            y_send(n).start()

    for q in range(4):
        ag_own(q)
    rest.wait()

    def add_rows(i, carry):
        block = abuf[pl.ds(pl.multiple_of(i * 64, 64), 64), :].astype(F32)
        return carry + jnp.sum(block.reshape(8, 8, width), axis=0)

    sums = lax.fori_loop(0, tokens // 64, add_rows, jnp.zeros((8, width), F32))
    to_tile(jnp.sum(sums, axis=0, keepdims=True), mz.at[z])


    exchange_start(mz, z, NZ, mz_s, mz_r, at_z)
    exchange_wait(mz, z, NZ, mz_s, mz_r, at_z)
    mx[x] = slot_sum(mz, NZ)
    exchange_start(mx, x, NX, mx_s, mx_r, at_x)
    forward(0)
    exchange_wait(mx, x, NX, mx_s, mx_r, at_x)
    my[yh] = slot_sum(mx, NX)
    exchange_start(my, yh, NYH, my_s, my_r, at_h)
    ag_own(4)
    forward(1)
    exchange_wait(my, yh, NYH, my_s, my_r, at_h)
    mean = slot_sum(my, NYH) / total
    mf[feat] = mean
    exchange_start(mf, feat, NF, mf_s, mf_r, at_f)
    for i in range(8):
        mrow[:, 128 * i : 128 * (i + 1)] = mean[i : i + 1, :]

    def center(i, carry):
        at = pl.ds(pl.multiple_of(i * 64, 64), 64)
        cbuf[at, :] = (abuf[at, :].astype(F32) - mrow[...]).astype(BF16)
        return carry

    lax.fori_loop(0, tokens // 64, center, 0)
    ag_own(5)
    forward(2)
    forward(3)

    exchange_wait(mf, feat, NF, mf_s, mf_r, at_f)
    for f in range(NF):
        value = jnp.where(pick, mf[f, 0:1, :], 0.0)
        mcol[f] = jnp.broadcast_to(jnp.sum(value, axis=1, keepdims=True), (PANEL, PANEL))

    ag_own(6)
    forward(4)
    share(0)
    share(1)
    ag_own(7)
    compute(0)
    forward(5)
    share(2)
    compute(1)

    tags.wait()
    classes = lax.broadcasted_iota(jnp.int32, (16, tokens), 0)
    onehot = jnp.where(classes == labels_ref[...], 1.0, 0.0).astype(BF16)

    def class_columns(n, carry):
        at = pl.ds(pl.multiple_of(n * 256, 256), 256)
        part = jnp.dot(onehot, cbuf[:, at], preferred_element_type=F32)
        for k in range(CLASSES):
            for i in range(2):
                crs[k, pl.ds(2 * n + i, 1), :] = part[k : k + 1, 128 * i : 128 * (i + 1)]
        return carry

    lax.fori_loop(0, width // 256, class_columns, 0)
    crr[z] = crs[z]
    for d in far_first(NZ):
        to = (z + d) % NZ
        remote(crs.at[to], crr.at[z], cr_s, cr_r, at_z(to)).start()

    forward(6)
    share(3)
    compute(2)
    xphase(0)
    share(4)
    compute(3)
    xphase(1)
    forward(7)
    zphase(0)
    exchange_wait(crr, z, NZ, cr_s, cr_r, at_z)
    cx[x] = slot_sum(crr, NZ)
    exchange_start(cx, x, NX, cx_s, cx_r, at_x)
    share(5)
    compute(4)
    xphase(2)
    zphase(1)
    exchange_wait(cx, x, NX, cx_s, cx_r, at_x)
    cy[yh] = slot_sum(cx, NX)
    exchange_start(cy, yh, NYH, cy_s, cy_r, at_h)
    share(6)
    compute(5)
    xphase(3)
    zphase(2)
    exchange_wait(cy, yh, NYH, cy_s, cy_r, at_h)
    cg[z] = slot_sum(cy, NYH)
    exchange_start(cg, z, NZ, cg_s, cg_r, at_z)
    share(7)
    compute(6)
    xphase(4)
    zphase(3)
    xphase(5)
    compute(7)
    zphase(4)
    xphase(6)
    zphase(5)
    xphase(7)
    zphase(6)
    yphase(0)
    yphase(1)
    yphase(2)
    yphase(3)
    yphase(4)
    exchange_wait(cg, z, NZ, cg_s, cg_r, at_z)
    for k in range(CLASSES):
        for i in range(8):
            cross_ref[k : k + 1, 128 * i : 128 * (i + 1)] = cg[k, i : i + 1, :] / total
    zphase(7)
    yphase(5)
    yphase(6)
    yphase(7)

    ag_drain()
    for m in range(6):
        sent = xr.at[:, m]
        remote(sent, sent, x_s.at[m], x_r.at[0, 0], dev(xx=right)).wait_send()
    remote(zr, zr, z_s, z_r.at[0], dev(zz=(z + 1) % NZ)).wait_send()
    remote(ysend, ysend, y_s, y_r, dev(hh=1 - yh)).wait_send()
    remote(yr, yr, y_s, y_r, dev(hh=1 - yh)).wait_recv()
    for n in range(Q // 2):
        value = (ykeep[n] + yr[n]) / (total - 1)
        for i in range(4):
            cov_ref[4 * n : 4 * n + 4, quarter * i : quarter * (i + 1)] = value[4 * i : 4 * i + 4, :]


def body(activations, labels):
    tokens, width = activations.shape
    dma = pltpu.SemaphoreType.DMA
    vm = pltpu.VMEM
    tile = (8, 128)
    scratch = [
        vm((tokens, width), BF16),
        vm((1, tokens), jnp.int32),
        vm((tokens, width), BF16),
        vm((Q, NC, NY, ROWS, tokens), BF16),
        vm((NF * ROWS, tokens), BF16),
        vm((Q, NX, NF * 4, width), F32),
        vm((Q, NX, NF * 4, width), BF16),
        vm((Q, 6, NF * 4, width // 2), BF16),
        vm((Q, NF, 16, width // 4), F32),
        vm((Q, NZ, 16, width // 4), BF16),
        vm((Q, NZ - 1, 16, width // 4), BF16),
        vm((Q // 2, 16, width // 4), F32),
        vm((Q // 2, 16, width // 4), F32),
        vm((Q // 2, 16, width // 4), F32),
        vm((NZ, *tile), F32),
        vm((NX, *tile), F32),
        vm((NYH, *tile), F32),
        vm((NF, *tile), F32),
        vm((1, width), F32),
        vm((NF, PANEL, PANEL), F32),
        vm((CLASSES, *tile), F32),
        vm((NZ, *tile), F32),
        vm((NX, *tile), F32),
        vm((NYH, *tile), F32),
        vm((NZ, *tile), F32),
        dma((3,)),
        dma((Q, NY)), dma((Q,)), dma((6,)),
        dma((6,)), dma((Q, 3)),
        dma(()), dma((Q,)),
        dma(()), dma(()),
    ] + [dma(())] * 16
    out_rows = NF * PANEL // (NZ * NYH * NX)
    return pl.pallas_call(
        kernel,
        out_shape=(
            jax.ShapeDtypeStruct((out_rows, width), F32),
            jax.ShapeDtypeStruct((CLASSES, width), F32),
        ),
        in_specs=[
            pl.BlockSpec(memory_space=pl.ANY),
            pl.BlockSpec(memory_space=pl.ANY),
        ],
        out_specs=(
            pl.BlockSpec(memory_space=pltpu.VMEM),
            pl.BlockSpec(memory_space=pltpu.VMEM),
        ),
        scratch_shapes=scratch,
        compiler_params=pltpu.CompilerParams(
            collective_id=0, has_side_effects=True, vmem_limit_bytes=60 * 2**20
        ),
        name="stats",
    )(activations, labels.reshape(1, tokens))


def solution(mesh):
    in_specs = (P("tok", "feat"), P("tok"))
    out_specs = (P("tok", "feat"), P(None, "feat"))
    return jax.shard_map(body, mesh=mesh, in_specs=in_specs, out_specs=out_specs, check_vma=False)
```

```python
import functools

import jax
import jax.numpy as jnp
from jax import lax
from jax.experimental import pallas as pl
from jax.experimental.pallas import tpu as pltpu
from jax.sharding import PartitionSpec as P

CLASSES = 8
PANEL = 128
NZ, NYH, NX = 8, 2, 4
NY, NC = 4, 2
NF = NY * NC
Q = 8
ROWS = PANEL // Q
MESH = pl.DeviceIdType.MESH
F32 = jnp.float32
BF16 = jnp.bfloat16


def chunk_column(row):
    quarter = row >> 5
    place = (row >> 2) & 7
    return 16 * place + 4 * quarter + (row & 3)


def fold(even, odd):
    low = lax.broadcasted_iota(jnp.int32, even.shape, 0) < 4
    return jnp.where(low, even, pltpu.roll(odd, 4, 0))


def fold_upper(even, odd):
    low = lax.broadcasted_iota(jnp.int32, even.shape, 0) < 4
    return jnp.where(low, pltpu.roll(even, 4, 0), odd)


def to_tile(row_value, ref):
    for i in range(8):
        ref[i : i + 1, :] = row_value[:, 128 * i : 128 * (i + 1)]


def kernel(
    act_hbm, labels_hbm, cov_ref, cross_ref,
    abuf, labels_ref, cbuf, pan, lhs, accf, xs, xr, zsum, zs, zr, ykeep, ysend, yr,
    mz, mx, my, mf, mrow, mcol, crs, crr, cx, cy, cg,
    load_sem, ag_r, ag_pr, ag_s, x_s, x_r, z_s, z_r, y_s, y_r,
    mz_s, mz_r, mx_s, mx_r, my_s, my_r, mf_s, mf_r,
    cr_s, cr_r, cx_s, cx_r, cy_s, cy_r, cg_s, cg_r,
):
    tokens, width = abuf.shape
    tok = lax.axis_index("tok")
    feat = lax.axis_index("feat")
    z = tok // (NYH * NX)
    yh = (tok // NX) % NYH
    x = tok % NX
    y = feat // NC
    c = feat % NC
    total = tokens * NZ * NYH * NX

    def dev(zz=None, hh=None, xx=None, ff=None):
        zz = z if zz is None else zz
        hh = yh if hh is None else hh
        xx = x if xx is None else xx
        ff = feat if ff is None else ff
        return {"tok": (zz * NYH + hh) * NX + xx, "feat": ff}

    def remote(src, dst, send, recv, device):
        return pltpu.make_async_remote_copy(
            src_ref=src, dst_ref=dst, send_sem=send, recv_sem=recv,
            device_id=device, device_id_type=MESH,
        )

    barrier = pltpu.get_barrier_semaphore()
    greet = [dev(zz=(z + d) % NZ) for d in (4, 3, 5, 2, 6, 1, 7)] + [dev(hh=1 - yh)]
    greet += [dev(ff=(feat + d) % NF) for d in range(1, NF)] + [dev(xx=(x + d) % NX) for d in range(1, NX)]
    for device in greet:
        pl.semaphore_signal(barrier, inc=1, device_id=device, device_id_type=MESH)

    first = pltpu.make_async_copy(
        act_hbm.at[:, pl.ds(0, PANEL)], abuf.at[:, pl.ds(0, PANEL)], load_sem.at[0])
    rest = pltpu.make_async_copy(
        act_hbm.at[:, pl.ds(PANEL, width - PANEL)],
        abuf.at[:, pl.ds(PANEL, width - PANEL)], load_sem.at[1])
    tags = pltpu.make_async_copy(labels_hbm, labels_ref, load_sem.at[2])
    first.start()
    rest.start()
    tags.start()

    first.wait()
    rows = lax.broadcasted_iota(jnp.int32, (PANEL, PANEL), 0)
    lanes = lax.broadcasted_iota(jnp.int32, (PANEL, PANEL), 1)
    pick = lanes == chunk_column(rows)
    select = jnp.where(pick, 1.0, 0.0).astype(BF16)
    for i in range(4):
        part = tokens // 4
        turned = lax.dot_general(
            select, abuf[i * part : (i + 1) * part, :PANEL],
            (((1,), (1,)), ((), ())), preferred_element_type=F32).astype(BF16)
        for q in range(Q):
            pan[q, c, y, :, i * part : (i + 1) * part] = turned[q * ROWS : (q + 1) * ROWS, :]

    rest.wait()

    def add_rows(i, carry):
        block = abuf[pl.ds(pl.multiple_of(i * 64, 64), 64), :].astype(F32)
        return carry + jnp.sum(block.reshape(8, 8, width), axis=0)

    sums = lax.fori_loop(0, tokens // 64, add_rows, jnp.zeros((8, width), F32))
    to_tile(jnp.sum(sums, axis=0, keepdims=True), mf.at[feat])


    pl.semaphore_wait(barrier, len(greet))

    def panel_copy(q, yy, to, n):
        to = jnp.clip(to, 0, NY - 1)
        return remote(
            pan.at[q, c, yy], pan.at[q, c, yy], ag_s.at[n], ag_r.at[q, yy], dev(ff=to * NC + c))

    def share_copy(q, yy):
        return remote(pan.at[q, c, yy], pan.at[q, c, yy], ag_s.at[5], ag_pr.at[q], dev(ff=y * NC + 1 - c))

    at_end = (y == 0) | (y == NY - 1)

    def send_own(q, steps, extra):
        for n, step in steps:
            @pl.when((y + step >= 0) & (y + step < NY) & extra)
            def _():
                panel_copy(q, y, y + step, n).start()

    def ag_far(q):
        send_own(q, ((0, 2), (1, -2)), at_end)

    def ag_near(q):
        send_own(q, ((0, 2), (1, -2)), jnp.logical_not(at_end))
        send_own(q, ((2, 1), (3, -1)), True)
        share_copy(q, y).start()

    def got(q, yy):
        panel_copy(q, yy, y, 0).wait_recv()
        share_copy(q, yy).start()

    def forward(q):
        @pl.when(y == 2)
        def _():
            got(q, 0)
            panel_copy(q, 0, 3, 4).start()

        @pl.when(y == 1)
        def _():
            got(q, 3)
            panel_copy(q, 3, 0, 4).start()

    def share(q):
        for step in (1, -1, 2, -2, 3, -3):
            inside = (y + step >= 0) & (y + step < NY)
            if abs(step) == 2:
                inside = inside & ((y == 0) | (y == NY - 1))

            @pl.when(inside)
            def _():
                got(q, y + step)

    def ag_recv_part(q):
        remote(pan.at[q, 1 - c], pan.at[q, 1 - c], ag_s.at[5], ag_pr.at[q], dev(ff=y * NC + 1 - c)).wait_recv()

    def ag_drain():
        own = pan.at[:, c, y]
        for n, step in enumerate((2, -2, 1, -1)):
            @pl.when((y + step >= 0) & (y + step < NY))
            def _():
                remote(own, own, ag_s.at[n], ag_r.at[0, 0], dev(ff=y * NC + 1 - c)).wait_send()

        @pl.when((y == 1) | (y == 2))
        def _():
            remote(own, own, ag_s.at[4], ag_r.at[0, 0], dev(ff=y * NC + 1 - c)).wait_send()

        shared = pan.at[:, c]
        remote(shared, shared, ag_s.at[5], ag_r.at[0, 0], dev(ff=y * NC + 1 - c)).wait_send()

    def far_first(n):
        return sorted(range(1, n), key=lambda d: -min(d, n - d))

    def exchange_start(buf, own, n, send, recv, where):
        for d in far_first(n):
            to = (own + d) % n
            remote(buf.at[own], buf.at[own], send, recv, where(to)).start()

    def exchange_wait(buf, own, n, send, recv, where):
        rest_of = buf.at[pl.ds(0, n - 1)]
        every = remote(rest_of, rest_of, send, recv, where((own + 1) % n))
        every.wait_recv()

    def exchange_sent(buf, n, send, recv, where):
        rest_of = buf.at[pl.ds(0, n - 1)]
        remote(rest_of, rest_of, send, recv, where(0)).wait_send()

    def at_z(to):
        return dev(zz=to)

    def at_x(to):
        return dev(xx=to)

    def at_h(to):
        return dev(hh=to)

    def at_f(to):
        return dev(ff=to)

    def slot_sum(buf, n):
        value = buf[0]
        for i in range(1, n):
            value = value + buf[i]
        return value

    half = width // 2
    quarter = width // 4
    side_a, side_b = pl.ds(0, half), pl.ds(half, half)

    def compute(q):
        ag_recv_part(q)
        for f in range(NF):
            block = pan[q, f % NC, f // NC].astype(F32) - mcol[f, q * ROWS : (q + 1) * ROWS, 0:1]
            lhs[f * ROWS : (f + 1) * ROWS, :] = block.astype(BF16)

        def columns(n, carry):
            at = pl.ds(pl.multiple_of(n * 256, 256), 256)
            acc = jnp.dot(lhs[...], cbuf[:, at], preferred_element_type=F32)
            acc = acc.reshape(NF // 2, 2, NX // 2, 8, 256)
            for xx in range(NX):
                join = fold_upper if xx % 2 else fold
                rows = [join(acc[i, 0, xx // 2], acc[i, 1, xx // 2]) for i in range(NF // 2)]
                slab = jnp.concatenate(rows, axis=0)
                accf[q, xx, :, at] = slab
                xs[q, xx, :, at] = slab.astype(BF16)
            return carry

        if q < Q - 1:
            lax.fori_loop(0, width // 256, columns, 0)
        else:
            lax.fori_loop(0, width // 512, columns, 0)
            x_copy(q, 0).start()
            x_copy(q, 3).start()
            lax.fori_loop(width // 512, width // 256, columns, 0)
            x_copy(q, 1).start()
            x_copy(q, 2).start()

    def xstart(q):
        for m in range(4):
            x_copy(q, m).start()

    right, left, across = (x + 1) % NX, (x + NX - 1) % NX, (x + 2) % NX

    def x_copy(q, m):
        slab = (across, across, right, left, right, left)[m]
        side = (side_a, side_b, side_b, side_a, side_a, side_b)[m]
        to = (right, left)[m % 2]
        return remote(xs.at[q, slab, :, side], xr.at[q, m], x_s.at[m], x_r.at[q, min(m, 2)], dev(xx=to))

    def xphase(q):
        for m, slab, side in ((4, right, side_a), (5, left, side_b)):
            x_copy(q, m - 4).wait_recv()
            xs[q, slab, :, side] = (accf[q, slab, :, side] + xr[q, m - 4].astype(F32)).astype(BF16)
            x_copy(q, m).start()

    def z_send(q, d):
        to = (z + d) % NZ
        return remote(zs.at[q, to], zr.at[q, d - 1], z_s, z_r.at[q], dev(zz=to))

    def zphase(q):
        last = xr.at[q, 2:6]
        remote(last, last, x_s.at[2], x_r.at[q, 2], dev(xx=right)).wait_recv()
        value_a = accf[q, x, :, side_a] + xr[q, 4].astype(F32) + xr[q, 3].astype(F32)
        value_b = accf[q, x, :, side_b] + xr[q, 2].astype(F32) + xr[q, 5].astype(F32)
        for f in range(NF):
            join = fold_upper if f % 2 else fold
            at = slice(f // 2 * 8, f // 2 * 8 + 8)
            packed = jnp.concatenate(
                [join(v[at, :quarter], v[at, quarter:]) for v in (value_a, value_b)], axis=0)
            zsum[q, f] = packed
            zs[q, f] = packed.astype(BF16)
        for d in far_first(NZ):
            z_send(q, d).start()

    def y_send(n):
        return remote(ysend.at[n], yr.at[n], y_s, y_r, dev(hh=1 - yh))

    def yphase(q):
        remote(zr.at[q], zr.at[q], z_s, z_r.at[q], dev(zz=(z + 1) % NZ)).wait_recv()
        value = zsum[q, z]
        for d in range(NZ - 1):
            value = value + zr[q, d].astype(F32)
        n = q // 2

        @pl.when(yh == q % 2)
        def _():
            ykeep[n] = value

        @pl.when(yh != q % 2)
        def _():
            ysend[n] = value
            y_send(n).start()

    exchange_start(mf, feat, NF, mf_s, mf_r, at_f)
    ag_far(0)
    ag_near(0)
    ag_far(1)
    ag_near(1)
    ag_far(2)
    mz[z, :8, :] = mf[feat]
    exchange_wait(mf, feat, NF, mf_s, mf_r, at_f)
    for f in range(NF):
        mz[z, 8 + f : 9 + f, :] = mf[f, 0:1, :]
    exchange_start(mz, z, NZ, mz_s, mz_r, at_z)
    ag_near(2)
    ag_far(3)
    ag_near(3)
    exchange_wait(mz, z, NZ, mz_s, mz_r, at_z)
    mx[x] = slot_sum(mz, NZ)
    exchange_start(mx, x, NX, mx_s, mx_r, at_x)
    forward(0)
    forward(1)
    ag_far(4)
    ag_far(5)
    exchange_wait(mx, x, NX, mx_s, mx_r, at_x)
    my[yh] = slot_sum(mx, NX)
    exchange_start(my, yh, NYH, my_s, my_r, at_h)
    forward(2)
    forward(3)
    ag_near(4)
    ag_far(6)
    ag_far(7)
    share(0)
    exchange_wait(my, yh, NYH, my_s, my_r, at_h)
    mean = slot_sum(my, NYH) / total
    for i in range(8):
        mrow[:, 128 * i : 128 * (i + 1)] = mean[i : i + 1, :]

    def center(i, carry):
        at = pl.ds(pl.multiple_of(i * 64, 64), 64)
        cbuf[at, :] = (abuf[at, :].astype(F32) - mrow[...]).astype(BF16)
        return carry

    lax.fori_loop(0, tokens // 64, center, 0)
    forward(4)
    forward(5)
    ag_near(5)
    for f in range(NF):
        value = jnp.where(pick, mean[8 + f : 9 + f, :], 0.0)
        mcol[f] = jnp.broadcast_to(jnp.sum(value, axis=1, keepdims=True), (PANEL, PANEL))

    share(1)
    compute(0)
    xstart(0)
    forward(6)
    ag_near(6)
    ag_near(7)
    share(2)
    compute(1)
    xstart(1)
    share(3)
    compute(2)
    xphase(0)
    xstart(2)
    forward(7)
    share(4)
    compute(3)
    xphase(1)
    xstart(3)
    tags.wait()
    classes = lax.broadcasted_iota(jnp.int32, (16, tokens), 0)
    onehot = jnp.where(classes == labels_ref[...], 1.0, 0.0).astype(BF16)

    def class_columns(n, carry):
        at = pl.ds(pl.multiple_of(n * 256, 256), 256)
        part = jnp.dot(onehot, cbuf[:, at], preferred_element_type=F32)
        for k in range(CLASSES):
            for i in range(2):
                crs[k, pl.ds(2 * n + i, 1), :] = part[k : k + 1, 128 * i : 128 * (i + 1)]
        return carry

    lax.fori_loop(0, width // 256, class_columns, 0)
    crr[z] = crs[z]
    for d in far_first(NZ):
        to = (z + d) % NZ
        remote(crs.at[to], crr.at[z], cr_s, cr_r, at_z(to)).start()

    share(5)
    compute(4)
    xphase(2)
    xstart(4)
    zphase(0)
    compute(5)
    xphase(3)
    xstart(5)
    zphase(1)
    exchange_wait(crr, z, NZ, cr_s, cr_r, at_z)
    cx[x] = slot_sum(crr, NZ)
    exchange_start(cx, x, NX, cx_s, cx_r, at_x)
    share(6)
    compute(6)
    xphase(4)
    xstart(6)
    zphase(2)
    zphase(3)
    xphase(5)
    exchange_wait(cx, x, NX, cx_s, cx_r, at_x)
    cy[yh] = slot_sum(cx, NX)
    exchange_start(cy, yh, NYH, cy_s, cy_r, at_h)
    share(7)
    compute(7)
    xphase(6)
    zphase(4)
    zphase(5)
    yphase(0)
    yphase(1)
    xphase(7)
    zphase(6)
    yphase(2)
    yphase(3)
    exchange_wait(cy, yh, NYH, cy_s, cy_r, at_h)
    cg[z] = slot_sum(cy, NYH)
    exchange_start(cg, z, NZ, cg_s, cg_r, at_z)
    zphase(7)
    yphase(4)
    yphase(5)
    yphase(6)
    yphase(7)
    exchange_wait(cg, z, NZ, cg_s, cg_r, at_z)
    for k in range(CLASSES):
        for i in range(8):
            cross_ref[k : k + 1, 128 * i : 128 * (i + 1)] = cg[k, i : i + 1, :] / total
    ag_drain()
    exchange_sent(mf, NF, mf_s, mf_r, at_f)
    exchange_sent(mz, NZ, mz_s, mz_r, at_z)
    exchange_sent(mx, NX, mx_s, mx_r, at_x)
    exchange_sent(my, NYH, my_s, my_r, at_h)
    exchange_sent(crr, NZ, cr_s, cr_r, at_z)
    exchange_sent(cx, NX, cx_s, cx_r, at_x)
    exchange_sent(cy, NYH, cy_s, cy_r, at_h)
    exchange_sent(cg, NZ, cg_s, cg_r, at_z)
    for m in range(6):
        sent = xr.at[:, m]
        remote(sent, sent, x_s.at[m], x_r.at[0, 0], dev(xx=right)).wait_send()
    remote(zr, zr, z_s, z_r.at[0], dev(zz=(z + 1) % NZ)).wait_send()
    remote(ysend, ysend, y_s, y_r, dev(hh=1 - yh)).wait_send()
    remote(yr, yr, y_s, y_r, dev(hh=1 - yh)).wait_recv()
    for n in range(Q // 2):
        value = (ykeep[n] + yr[n]) / (total - 1)
        for i in range(4):
            cov_ref[4 * n : 4 * n + 4, quarter * i : quarter * (i + 1)] = value[4 * i : 4 * i + 4, :]


def body(activations, labels):
    tokens, width = activations.shape
    dma = pltpu.SemaphoreType.DMA
    vm = pltpu.VMEM
    tile = (8, 128)
    scratch = [
        vm((tokens, width), BF16),
        vm((1, tokens), jnp.int32),
        vm((tokens, width), BF16),
        vm((Q, NC, NY, ROWS, tokens), BF16),
        vm((NF * ROWS, tokens), BF16),
        vm((Q, NX, NF * 4, width), F32),
        vm((Q, NX, NF * 4, width), BF16),
        vm((Q, 6, NF * 4, width // 2), BF16),
        vm((Q, NF, 16, width // 4), F32),
        vm((Q, NZ, 16, width // 4), BF16),
        vm((Q, NZ - 1, 16, width // 4), BF16),
        vm((Q // 2, 16, width // 4), F32),
        vm((Q // 2, 16, width // 4), F32),
        vm((Q // 2, 16, width // 4), F32),
        vm((NZ, 16, 128), F32),
        vm((NX, 16, 128), F32),
        vm((NYH, 16, 128), F32),
        vm((NF, *tile), F32),
        vm((1, width), F32),
        vm((NF, PANEL, PANEL), F32),
        vm((CLASSES, *tile), F32),
        vm((NZ, *tile), F32),
        vm((NX, *tile), F32),
        vm((NYH, *tile), F32),
        vm((NZ, *tile), F32),
        dma((3,)),
        dma((Q, NY)), dma((Q,)), dma((6,)),
        dma((6,)), dma((Q, 3)),
        dma(()), dma((Q,)),
        dma(()), dma(()),
    ] + [dma(())] * 16
    out_rows = NF * PANEL // (NZ * NYH * NX)
    return pl.pallas_call(
        kernel,
        out_shape=(
            jax.ShapeDtypeStruct((out_rows, width), F32),
            jax.ShapeDtypeStruct((CLASSES, width), F32),
        ),
        in_specs=[
            pl.BlockSpec(memory_space=pl.ANY),
            pl.BlockSpec(memory_space=pl.ANY),
        ],
        out_specs=(
            pl.BlockSpec(memory_space=pltpu.VMEM),
            pl.BlockSpec(memory_space=pltpu.VMEM),
        ),
        scratch_shapes=scratch,
        compiler_params=pltpu.CompilerParams(
            collective_id=0, has_side_effects=True, vmem_limit_bytes=60 * 2**20
        ),
        name="stats",
    )(activations, labels.reshape(1, tokens))


def solution(mesh):
    in_specs = (P("tok", "feat"), P("tok"))
    out_specs = (P("tok", "feat"), P(None, "feat"))
    return jax.shard_map(body, mesh=mesh, in_specs=in_specs, out_specs=out_specs, check_vma=False)
```

```python
import functools

import jax
import jax.numpy as jnp
from jax import lax
from jax.experimental import pallas as pl
from jax.experimental.pallas import tpu as pltpu
from jax.sharding import PartitionSpec as P

CLASSES = 8
PANEL = 128
NZ, NYH, NX = 8, 2, 4
NY, NC = 4, 2
NF = NY * NC
Q = 8
ROWS = PANEL // Q
MESH = pl.DeviceIdType.MESH
F32 = jnp.float32
BF16 = jnp.bfloat16


def chunk_column(row):
    quarter = row >> 5
    place = (row >> 2) & 7
    return 16 * place + 4 * quarter + (row & 3)


def fold(even, odd):
    low = lax.broadcasted_iota(jnp.int32, even.shape, 0) < 4
    return jnp.where(low, even, pltpu.roll(odd, 4, 0))


def fold_upper(even, odd):
    low = lax.broadcasted_iota(jnp.int32, even.shape, 0) < 4
    return jnp.where(low, pltpu.roll(even, 4, 0), odd)


def to_tile(row_value, ref):
    for i in range(8):
        ref[i : i + 1, :] = row_value[:, 128 * i : 128 * (i + 1)]


def kernel(
    act_hbm, labels_hbm, cov_ref, cross_ref,
    abuf, labels_ref, cbuf, pan, lhs, accf, xs, xr, zsum, zs, zr, ykeep, ysend, yr,
    mz, mx, my, mf, mrow, mcol, crs, crr, cx, cy, cg,
    load_sem, ag_r, ag_pr, ag_s, x_s, x_r, z_s, z_r, y_s, y_r,
    mz_s, mz_r, mx_s, mx_r, my_s, my_r, mf_s, mf_r,
    cr_s, cr_r, cx_s, cx_r, cy_s, cy_r, cg_s, cg_r,
):
    tokens, width = abuf.shape
    tok = lax.axis_index("tok")
    feat = lax.axis_index("feat")
    z = tok // (NYH * NX)
    yh = (tok // NX) % NYH
    x = tok % NX
    y = feat // NC
    c = feat % NC
    total = tokens * NZ * NYH * NX

    def dev(zz=None, hh=None, xx=None, ff=None):
        zz = z if zz is None else zz
        hh = yh if hh is None else hh
        xx = x if xx is None else xx
        ff = feat if ff is None else ff
        return {"tok": (zz * NYH + hh) * NX + xx, "feat": ff}

    def remote(src, dst, send, recv, device):
        return pltpu.make_async_remote_copy(
            src_ref=src, dst_ref=dst, send_sem=send, recv_sem=recv,
            device_id=device, device_id_type=MESH,
        )

    barrier = pltpu.get_barrier_semaphore()
    greet = [dev(zz=(z + d) % NZ) for d in (4, 3, 5, 2, 6, 1, 7)] + [dev(hh=1 - yh)]
    greet += [dev(ff=(feat + d) % NF) for d in range(1, NF)] + [dev(xx=(x + d) % NX) for d in range(1, NX)]
    for device in greet:
        pl.semaphore_signal(barrier, inc=1, device_id=device, device_id_type=MESH)

    first = pltpu.make_async_copy(
        act_hbm.at[:, pl.ds(0, PANEL)], abuf.at[:, pl.ds(0, PANEL)], load_sem.at[0])
    rest = pltpu.make_async_copy(
        act_hbm.at[:, pl.ds(PANEL, width - PANEL)],
        abuf.at[:, pl.ds(PANEL, width - PANEL)], load_sem.at[1])
    tags = pltpu.make_async_copy(labels_hbm, labels_ref, load_sem.at[2])
    first.start()
    rest.start()
    tags.start()

    first.wait()
    rows = lax.broadcasted_iota(jnp.int32, (PANEL, PANEL), 0)
    lanes = lax.broadcasted_iota(jnp.int32, (PANEL, PANEL), 1)
    pick = lanes == chunk_column(rows)
    select = jnp.where(pick, 1.0, 0.0).astype(BF16)
    for i in range(4):
        part = tokens // 4
        turned = lax.dot_general(
            select, abuf[i * part : (i + 1) * part, :PANEL],
            (((1,), (1,)), ((), ())), preferred_element_type=F32).astype(BF16)
        for q in range(Q):
            pan[q, c, y, :, i * part : (i + 1) * part] = turned[q * ROWS : (q + 1) * ROWS, :]

    rest.wait()

    def add_rows(i, carry):
        block = abuf[pl.ds(pl.multiple_of(i * 64, 64), 64), :].astype(F32)
        return carry + jnp.sum(block.reshape(8, 8, width), axis=0)

    sums = lax.fori_loop(0, tokens // 64, add_rows, jnp.zeros((8, width), F32))
    to_tile(jnp.sum(sums, axis=0, keepdims=True), mf.at[feat])


    pl.semaphore_wait(barrier, len(greet))

    def panel_copy(q, yy, to, n):
        to = jnp.clip(to, 0, NY - 1)
        return remote(
            pan.at[q, c, yy], pan.at[q, c, yy], ag_s.at[n], ag_r.at[q, yy], dev(ff=to * NC + c))

    def share_copy(q, yy):
        return remote(pan.at[q, c, yy], pan.at[q, c, yy], ag_s.at[5], ag_pr.at[q], dev(ff=y * NC + 1 - c))

    at_end = (y == 0) | (y == NY - 1)

    def send_own(q, steps, extra):
        for n, step in steps:
            @pl.when((y + step >= 0) & (y + step < NY) & extra)
            def _():
                panel_copy(q, y, y + step, n).start()

    def ag_far(q):
        send_own(q, ((0, 2), (1, -2)), at_end)

    def ag_near(q):
        send_own(q, ((0, 2), (1, -2)), jnp.logical_not(at_end))
        send_own(q, ((2, 1), (3, -1)), True)
        share_copy(q, y).start()

    def got(q, yy):
        panel_copy(q, yy, y, 0).wait_recv()
        share_copy(q, yy).start()

    def forward(q):
        @pl.when(y == 2)
        def _():
            got(q, 0)
            panel_copy(q, 0, 3, 4).start()

        @pl.when(y == 1)
        def _():
            got(q, 3)
            panel_copy(q, 3, 0, 4).start()

    def share(q):
        for step in (1, -1, 2, -2, 3, -3):
            inside = (y + step >= 0) & (y + step < NY)
            if abs(step) == 2:
                inside = inside & ((y == 0) | (y == NY - 1))

            @pl.when(inside)
            def _():
                got(q, y + step)

    def ag_recv_part(q):
        remote(pan.at[q, 1 - c], pan.at[q, 1 - c], ag_s.at[5], ag_pr.at[q], dev(ff=y * NC + 1 - c)).wait_recv()

    def ag_drain():
        own = pan.at[:, c, y]
        for n, step in enumerate((2, -2, 1, -1)):
            @pl.when((y + step >= 0) & (y + step < NY))
            def _():
                remote(own, own, ag_s.at[n], ag_r.at[0, 0], dev(ff=y * NC + 1 - c)).wait_send()

        @pl.when((y == 1) | (y == 2))
        def _():
            remote(own, own, ag_s.at[4], ag_r.at[0, 0], dev(ff=y * NC + 1 - c)).wait_send()

        shared = pan.at[:, c]
        remote(shared, shared, ag_s.at[5], ag_r.at[0, 0], dev(ff=y * NC + 1 - c)).wait_send()

    def far_first(n):
        return sorted(range(1, n), key=lambda d: -min(d, n - d))

    def exchange_start(buf, own, n, send, recv, where):
        for d in far_first(n):
            to = (own + d) % n
            remote(buf.at[own], buf.at[own], send, recv, where(to)).start()

    def exchange_wait(buf, own, n, send, recv, where):
        rest_of = buf.at[pl.ds(0, n - 1)]
        every = remote(rest_of, rest_of, send, recv, where((own + 1) % n))
        every.wait_recv()

    def exchange_sent(buf, n, send, recv, where):
        rest_of = buf.at[pl.ds(0, n - 1)]
        remote(rest_of, rest_of, send, recv, where(0)).wait_send()

    def at_z(to):
        return dev(zz=to)

    def at_x(to):
        return dev(xx=to)

    def at_h(to):
        return dev(hh=to)

    def at_f(to):
        return dev(ff=to)

    def slot_sum(buf, n):
        value = buf[0]
        for i in range(1, n):
            value = value + buf[i]
        return value

    half = width // 2
    quarter = width // 4
    side_a, side_b = pl.ds(0, half), pl.ds(half, half)

    def compute(q):
        ag_recv_part(q)
        for f in range(NF):
            block = pan[q, f % NC, f // NC].astype(F32) - mcol[f, q * ROWS : (q + 1) * ROWS, 0:1]
            lhs[f * ROWS : (f + 1) * ROWS, :] = block.astype(BF16)

        def columns(n, carry):
            at = pl.ds(pl.multiple_of(n * 256, 256), 256)
            acc = jnp.dot(lhs[...], cbuf[:, at], preferred_element_type=F32)
            acc = acc.reshape(NF // 2, 2, NX // 2, 8, 256)
            for xx in range(NX):
                join = fold_upper if xx % 2 else fold
                rows = [join(acc[i, 0, xx // 2], acc[i, 1, xx // 2]) for i in range(NF // 2)]
                slab = jnp.concatenate(rows, axis=0)
                accf[q, xx, :, at] = slab
                xs[q, xx, :, at] = slab.astype(BF16)
            return carry

        if q < Q - 1:
            lax.fori_loop(0, width // 256, columns, 0)
        else:
            lax.fori_loop(0, width // 512, columns, 0)
            x_copy(q, 0).start()
            x_copy(q, 3).start()
            lax.fori_loop(width // 512, width // 256, columns, 0)
            x_copy(q, 1).start()
            x_copy(q, 2).start()

    def xstart(q):
        for m in range(4):
            x_copy(q, m).start()

    right, left, across = (x + 1) % NX, (x + NX - 1) % NX, (x + 2) % NX

    def x_copy(q, m):
        slab = (across, across, right, left, right, left)[m]
        side = (side_a, side_b, side_b, side_a, side_a, side_b)[m]
        to = (right, left)[m % 2]
        return remote(xs.at[q, slab, :, side], xr.at[q, m], x_s.at[m], x_r.at[q, min(m, 2)], dev(xx=to))

    def xphase(q):
        for m, slab, side in ((4, right, side_a), (5, left, side_b)):
            x_copy(q, m - 4).wait_recv()
            xs[q, slab, :, side] = (accf[q, slab, :, side] + xr[q, m - 4].astype(F32)).astype(BF16)
            x_copy(q, m).start()

    def z_send(q, d):
        to = (z + d) % NZ
        return remote(zs.at[q, to], zr.at[q, d - 1], z_s, z_r.at[q], dev(zz=to))

    def zphase(q):
        last = xr.at[q, 2:6]
        remote(last, last, x_s.at[2], x_r.at[q, 2], dev(xx=right)).wait_recv()
        value_a = accf[q, x, :, side_a] + xr[q, 4].astype(F32) + xr[q, 3].astype(F32)
        value_b = accf[q, x, :, side_b] + xr[q, 2].astype(F32) + xr[q, 5].astype(F32)
        for f in range(NF):
            join = fold_upper if f % 2 else fold
            at = slice(f // 2 * 8, f // 2 * 8 + 8)
            packed = jnp.concatenate(
                [join(v[at, :quarter], v[at, quarter:]) for v in (value_a, value_b)], axis=0)
            zsum[q, f] = packed
            zs[q, f] = packed.astype(BF16)
        for d in far_first(NZ):
            z_send(q, d).start()

    def y_send(n):
        return remote(ysend.at[n], yr.at[n], y_s, y_r, dev(hh=1 - yh))

    def yphase(q):
        remote(zr.at[q], zr.at[q], z_s, z_r.at[q], dev(zz=(z + 1) % NZ)).wait_recv()
        value = zsum[q, z]
        for d in range(NZ - 1):
            value = value + zr[q, d].astype(F32)
        n = q // 2

        @pl.when(yh == q % 2)
        def _():
            ykeep[n] = value

        @pl.when(yh != q % 2)
        def _():
            ysend[n] = value
            y_send(n).start()

    exchange_start(mf, feat, NF, mf_s, mf_r, at_f)
    ag_far(0)
    ag_near(0)
    ag_far(1)
    ag_near(1)
    ag_far(2)
    mz[z, :8, :] = mf[feat]
    exchange_wait(mf, feat, NF, mf_s, mf_r, at_f)
    for f in range(NF):
        mz[z, 8 + f : 9 + f, :] = mf[f, 0:1, :]
    exchange_start(mz, z, NZ, mz_s, mz_r, at_z)
    ag_near(2)
    ag_far(3)
    ag_near(3)
    exchange_wait(mz, z, NZ, mz_s, mz_r, at_z)
    mx[x] = slot_sum(mz, NZ)
    exchange_start(mx, x, NX, mx_s, mx_r, at_x)
    forward(0)
    forward(1)
    ag_far(4)
    ag_far(5)
    exchange_wait(mx, x, NX, mx_s, mx_r, at_x)
    my[yh] = slot_sum(mx, NX)
    exchange_start(my, yh, NYH, my_s, my_r, at_h)
    forward(2)
    forward(3)
    ag_near(4)
    ag_far(6)
    ag_far(7)
    share(0)
    exchange_wait(my, yh, NYH, my_s, my_r, at_h)
    mean = slot_sum(my, NYH) / total
    for i in range(8):
        mrow[:, 128 * i : 128 * (i + 1)] = mean[i : i + 1, :]

    def center(i, carry):
        at = pl.ds(pl.multiple_of(i * 64, 64), 64)
        cbuf[at, :] = (abuf[at, :].astype(F32) - mrow[...]).astype(BF16)
        return carry

    lax.fori_loop(0, tokens // 64, center, 0)
    forward(4)
    forward(5)
    ag_near(5)
    for f in range(NF):
        value = jnp.where(pick, mean[8 + f : 9 + f, :], 0.0)
        mcol[f] = jnp.broadcast_to(jnp.sum(value, axis=1, keepdims=True), (PANEL, PANEL))

    share(1)
    compute(0)
    xstart(0)
    forward(6)
    ag_near(6)
    ag_near(7)
    share(2)
    compute(1)
    xstart(1)
    share(3)
    compute(2)
    xphase(0)
    xstart(2)
    forward(7)
    share(4)
    compute(3)
    xphase(1)
    xstart(3)
    tags.wait()
    classes = lax.broadcasted_iota(jnp.int32, (16, tokens), 0)
    onehot = jnp.where(classes == labels_ref[...], 1.0, 0.0).astype(BF16)

    def class_columns(n, carry):
        at = pl.ds(pl.multiple_of(n * 256, 256), 256)
        part = jnp.dot(onehot, cbuf[:, at], preferred_element_type=F32)
        for k in range(CLASSES):
            for i in range(2):
                crs[k, pl.ds(2 * n + i, 1), :] = part[k : k + 1, 128 * i : 128 * (i + 1)]
        return carry

    lax.fori_loop(0, width // 256, class_columns, 0)
    crr[z] = crs[z]
    for d in far_first(NZ):
        to = (z + d) % NZ
        remote(crs.at[to], crr.at[z], cr_s, cr_r, at_z(to)).start()

    share(5)
    compute(4)
    xphase(2)
    xstart(4)
    zphase(0)
    compute(5)
    xphase(3)
    xstart(5)
    zphase(1)
    share(6)
    compute(6)
    xphase(4)
    xstart(6)
    zphase(2)
    share(7)
    exchange_wait(crr, z, NZ, cr_s, cr_r, at_z)
    cx[x] = slot_sum(crr, NZ)
    exchange_start(cx, x, NX, cx_s, cx_r, at_x)
    xphase(5)
    zphase(3)
    compute(7)
    xphase(6)
    zphase(4)
    exchange_wait(cx, x, NX, cx_s, cx_r, at_x)
    cy[yh] = slot_sum(cx, NX)
    exchange_start(cy, yh, NYH, cy_s, cy_r, at_h)
    yphase(0)
    yphase(1)
    zphase(5)
    xphase(7)
    zphase(6)
    yphase(2)
    zphase(7)
    exchange_wait(cy, yh, NYH, cy_s, cy_r, at_h)
    cg[z] = slot_sum(cy, NYH)
    exchange_start(cg, z, NZ, cg_s, cg_r, at_z)
    yphase(3)
    yphase(4)
    yphase(5)
    yphase(6)
    yphase(7)
    exchange_wait(cg, z, NZ, cg_s, cg_r, at_z)
    for k in range(CLASSES):
        for i in range(8):
            cross_ref[k : k + 1, 128 * i : 128 * (i + 1)] = cg[k, i : i + 1, :] / total
    ag_drain()
    exchange_sent(mf, NF, mf_s, mf_r, at_f)
    exchange_sent(mz, NZ, mz_s, mz_r, at_z)
    exchange_sent(mx, NX, mx_s, mx_r, at_x)
    exchange_sent(my, NYH, my_s, my_r, at_h)
    exchange_sent(crr, NZ, cr_s, cr_r, at_z)
    exchange_sent(cx, NX, cx_s, cx_r, at_x)
    exchange_sent(cy, NYH, cy_s, cy_r, at_h)
    exchange_sent(cg, NZ, cg_s, cg_r, at_z)
    for m in range(6):
        sent = xr.at[:, m]
        remote(sent, sent, x_s.at[m], x_r.at[0, 0], dev(xx=right)).wait_send()
    remote(zr, zr, z_s, z_r.at[0], dev(zz=(z + 1) % NZ)).wait_send()
    remote(ysend, ysend, y_s, y_r, dev(hh=1 - yh)).wait_send()
    remote(yr, yr, y_s, y_r, dev(hh=1 - yh)).wait_recv()
    for n in range(Q // 2):
        value = (ykeep[n] + yr[n]) / (total - 1)
        for i in range(4):
            cov_ref[4 * n : 4 * n + 4, quarter * i : quarter * (i + 1)] = value[4 * i : 4 * i + 4, :]


def body(activations, labels):
    tokens, width = activations.shape
    dma = pltpu.SemaphoreType.DMA
    vm = pltpu.VMEM
    tile = (8, 128)
    scratch = [
        vm((tokens, width), BF16),
        vm((1, tokens), jnp.int32),
        vm((tokens, width), BF16),
        vm((Q, NC, NY, ROWS, tokens), BF16),
        vm((NF * ROWS, tokens), BF16),
        vm((Q, NX, NF * 4, width), F32),
        vm((Q, NX, NF * 4, width), BF16),
        vm((Q, 6, NF * 4, width // 2), BF16),
        vm((Q, NF, 16, width // 4), F32),
        vm((Q, NZ, 16, width // 4), BF16),
        vm((Q, NZ - 1, 16, width // 4), BF16),
        vm((Q // 2, 16, width // 4), F32),
        vm((Q // 2, 16, width // 4), F32),
        vm((Q // 2, 16, width // 4), F32),
        vm((NZ, 16, 128), F32),
        vm((NX, 16, 128), F32),
        vm((NYH, 16, 128), F32),
        vm((NF, *tile), F32),
        vm((1, width), F32),
        vm((NF, PANEL, PANEL), F32),
        vm((CLASSES, *tile), F32),
        vm((NZ, *tile), F32),
        vm((NX, *tile), F32),
        vm((NYH, *tile), F32),
        vm((NZ, *tile), F32),
        dma((3,)),
        dma((Q, NY)), dma((Q,)), dma((6,)),
        dma((6,)), dma((Q, 3)),
        dma(()), dma((Q,)),
        dma(()), dma(()),
    ] + [dma(())] * 16
    out_rows = NF * PANEL // (NZ * NYH * NX)
    return pl.pallas_call(
        kernel,
        out_shape=(
            jax.ShapeDtypeStruct((out_rows, width), F32),
            jax.ShapeDtypeStruct((CLASSES, width), F32),
        ),
        in_specs=[
            pl.BlockSpec(memory_space=pl.ANY),
            pl.BlockSpec(memory_space=pl.ANY),
        ],
        out_specs=(
            pl.BlockSpec(memory_space=pltpu.VMEM),
            pl.BlockSpec(memory_space=pltpu.VMEM),
        ),
        scratch_shapes=scratch,
        compiler_params=pltpu.CompilerParams(
            collective_id=0, has_side_effects=True, vmem_limit_bytes=60 * 2**20
        ),
        name="stats",
    )(activations, labels.reshape(1, tokens))


def solution(mesh):
    in_specs = (P("tok", "feat"), P("tok"))
    out_specs = (P("tok", "feat"), P(None, "feat"))
    return jax.shard_map(body, mesh=mesh, in_specs=in_specs, out_specs=out_specs, check_vma=False)
```

```python
import functools

import jax
import jax.numpy as jnp
from jax import lax
from jax.experimental import pallas as pl
from jax.experimental.pallas import tpu as pltpu
from jax.sharding import PartitionSpec as P

CLASSES = 8
PANEL = 128
NZ, NYH, NX = 8, 2, 4
NY, NC = 4, 2
NF = NY * NC
Q = 8
ROWS = PANEL // Q
MESH = pl.DeviceIdType.MESH
F32 = jnp.float32
BF16 = jnp.bfloat16


def chunk_column(row):
    quarter = row >> 5
    place = (row >> 2) & 7
    return 16 * place + 4 * quarter + (row & 3)


def fold(even, odd):
    low = lax.broadcasted_iota(jnp.int32, even.shape, 0) < 4
    return jnp.where(low, even, pltpu.roll(odd, 4, 0))


def fold_upper(even, odd):
    low = lax.broadcasted_iota(jnp.int32, even.shape, 0) < 4
    return jnp.where(low, pltpu.roll(even, 4, 0), odd)


def to_tile(row_value, ref):
    for i in range(8):
        ref[i : i + 1, :] = row_value[:, 128 * i : 128 * (i + 1)]


def kernel(
    act_hbm, labels_hbm, cov_out, cross_out,
    abuf, labels_ref, cbuf, pan, lhs, accf, xs, xr, zsum, zs, zr, ykeep, ysend, yr,
    mz, mx, my, mf, mrow, mcol, crs, crr, cx, cy, cg, cov_ref, cross_ref, out_sem,
    load_sem, ag_r, ag_pr, ag_s, x_s, x_r, z_s, z_r, y_s, y_r,
    mz_s, mz_r, mx_s, mx_r, my_s, my_r, mf_s, mf_r,
    cr_s, cr_r, cx_s, cx_r, cy_s, cy_r, cg_s, cg_r,
):
    tokens, width = abuf.shape
    tok = lax.axis_index("tok")
    feat = lax.axis_index("feat")
    z = tok // (NYH * NX)
    yh = (tok // NX) % NYH
    x = tok % NX
    y = feat // NC
    c = feat % NC
    total = tokens * NZ * NYH * NX

    def dev(zz=None, hh=None, xx=None, ff=None):
        zz = z if zz is None else zz
        hh = yh if hh is None else hh
        xx = x if xx is None else xx
        ff = feat if ff is None else ff
        return {"tok": (zz * NYH + hh) * NX + xx, "feat": ff}

    def remote(src, dst, send, recv, device):
        return pltpu.make_async_remote_copy(
            src_ref=src, dst_ref=dst, send_sem=send, recv_sem=recv,
            device_id=device, device_id_type=MESH,
        )

    first = pltpu.make_async_copy(
        act_hbm.at[:, pl.ds(0, PANEL)], abuf.at[:, pl.ds(0, PANEL)], load_sem.at[0])
    rest = pltpu.make_async_copy(
        act_hbm.at[:, pl.ds(PANEL, width - PANEL)],
        abuf.at[:, pl.ds(PANEL, width - PANEL)], load_sem.at[1])
    tags = pltpu.make_async_copy(labels_hbm, labels_ref, load_sem.at[2])
    first.start()
    rest.start()
    tags.start()

    barrier = pltpu.get_barrier_semaphore()
    greet = [dev(zz=(z + d) % NZ) for d in (4, 3, 5, 2, 6, 1, 7)] + [dev(hh=1 - yh)]
    greet += [dev(ff=(feat + d) % NF) for d in range(1, NF)] + [dev(xx=(x + d) % NX) for d in range(1, NX)]
    for device in greet:
        pl.semaphore_signal(barrier, inc=1, device_id=device, device_id_type=MESH)

    first.wait()
    rows = lax.broadcasted_iota(jnp.int32, (PANEL, PANEL), 0)
    lanes = lax.broadcasted_iota(jnp.int32, (PANEL, PANEL), 1)
    pick = lanes == chunk_column(rows)
    select = jnp.where(pick, 1.0, 0.0).astype(BF16)
    for i in range(4):
        part = tokens // 4
        turned = lax.dot_general(
            select, abuf[i * part : (i + 1) * part, :PANEL],
            (((1,), (1,)), ((), ())), preferred_element_type=F32).astype(BF16)
        for q in range(Q):
            pan[q, c, y, :, i * part : (i + 1) * part] = turned[q * ROWS : (q + 1) * ROWS, :]

    rest.wait()

    def add_rows(i, carry):
        block = abuf[pl.ds(pl.multiple_of(i * 64, 64), 64), :].astype(F32)
        return carry + jnp.sum(block.reshape(8, 8, width), axis=0)

    sums = lax.fori_loop(0, tokens // 64, add_rows, jnp.zeros((8, width), F32))
    to_tile(jnp.sum(sums, axis=0, keepdims=True), mf.at[feat])


    pl.semaphore_wait(barrier, len(greet))

    def panel_copy(q, yy, to, n):
        to = jnp.clip(to, 0, NY - 1)
        return remote(
            pan.at[q, c, yy], pan.at[q, c, yy], ag_s.at[n], ag_r.at[q, yy], dev(ff=to * NC + c))

    def share_copy(q, yy):
        return remote(pan.at[q, c, yy], pan.at[q, c, yy], ag_s.at[5], ag_pr.at[q], dev(ff=y * NC + 1 - c))

    at_end = (y == 0) | (y == NY - 1)

    def send_own(q, steps, extra):
        for n, step in steps:
            @pl.when((y + step >= 0) & (y + step < NY) & extra)
            def _():
                panel_copy(q, y, y + step, n).start()

    def ag_far(q):
        send_own(q, ((0, 2), (1, -2)), at_end)

    def ag_near(q):
        send_own(q, ((0, 2), (1, -2)), jnp.logical_not(at_end))
        send_own(q, ((2, 1), (3, -1)), True)
        share_copy(q, y).start()

    def got(q, yy):
        panel_copy(q, yy, y, 0).wait_recv()
        share_copy(q, yy).start()

    def forward(q):
        @pl.when(y == 2)
        def _():
            got(q, 0)
            panel_copy(q, 0, 3, 4).start()

        @pl.when(y == 1)
        def _():
            got(q, 3)
            panel_copy(q, 3, 0, 4).start()

    def share(q):
        for step in (1, -1, 2, -2, 3, -3):
            inside = (y + step >= 0) & (y + step < NY)
            if abs(step) == 2:
                inside = inside & ((y == 0) | (y == NY - 1))

            @pl.when(inside)
            def _():
                got(q, y + step)

    def ag_recv_part(q):
        remote(pan.at[q, 1 - c], pan.at[q, 1 - c], ag_s.at[5], ag_pr.at[q], dev(ff=y * NC + 1 - c)).wait_recv()

    def ag_drain():
        own = pan.at[:, c, y]
        for n, step in enumerate((2, -2, 1, -1)):
            @pl.when((y + step >= 0) & (y + step < NY))
            def _():
                remote(own, own, ag_s.at[n], ag_r.at[0, 0], dev(ff=y * NC + 1 - c)).wait_send()

        @pl.when((y == 1) | (y == 2))
        def _():
            remote(own, own, ag_s.at[4], ag_r.at[0, 0], dev(ff=y * NC + 1 - c)).wait_send()

        shared = pan.at[:, c]
        remote(shared, shared, ag_s.at[5], ag_r.at[0, 0], dev(ff=y * NC + 1 - c)).wait_send()

    def far_first(n):
        return sorted(range(1, n), key=lambda d: -min(d, n - d))

    def exchange_start(buf, own, n, send, recv, where):
        for d in far_first(n):
            to = (own + d) % n
            remote(buf.at[own], buf.at[own], send, recv, where(to)).start()

    def exchange_wait(buf, own, n, send, recv, where):
        rest_of = buf.at[pl.ds(0, n - 1)]
        every = remote(rest_of, rest_of, send, recv, where((own + 1) % n))
        every.wait_recv()

    def exchange_sent(buf, n, send, recv, where):
        rest_of = buf.at[pl.ds(0, n - 1)]
        remote(rest_of, rest_of, send, recv, where(0)).wait_send()

    def at_z(to):
        return dev(zz=to)

    def at_x(to):
        return dev(xx=to)

    def at_h(to):
        return dev(hh=to)

    def at_f(to):
        return dev(ff=to)

    def slot_sum(buf, n):
        value = buf[0]
        for i in range(1, n):
            value = value + buf[i]
        return value

    half = width // 2
    quarter = width // 4
    side_a, side_b = pl.ds(0, half), pl.ds(half, half)

    def compute(q):
        ag_recv_part(q)
        for f in range(NF):
            block = pan[q, f % NC, f // NC].astype(F32) - mcol[f, q * ROWS : (q + 1) * ROWS, 0:1]
            lhs[f * ROWS : (f + 1) * ROWS, :] = block.astype(BF16)

        def columns(n, carry):
            at = pl.ds(pl.multiple_of(n * 256, 256), 256)
            acc = jnp.dot(lhs[...], cbuf[:, at], preferred_element_type=F32)
            acc = acc.reshape(NF // 2, 2, NX // 2, 8, 256)
            for xx in range(NX):
                join = fold_upper if xx % 2 else fold
                rows = [join(acc[i, 0, xx // 2], acc[i, 1, xx // 2]) for i in range(NF // 2)]
                slab = jnp.concatenate(rows, axis=0)
                accf[q, xx, :, at] = slab
                xs[q, xx, :, at] = slab.astype(BF16)
            return carry

        if q < Q - 1:
            lax.fori_loop(0, width // 256, columns, 0)
        else:
            lax.fori_loop(0, width // 512, columns, 0)
            x_copy(q, 0).start()
            x_copy(q, 3).start()
            lax.fori_loop(width // 512, width // 256, columns, 0)
            x_copy(q, 1).start()
            x_copy(q, 2).start()

    def xstart(q):
        for m in range(4):
            x_copy(q, m).start()

    right, left, across = (x + 1) % NX, (x + NX - 1) % NX, (x + 2) % NX

    def x_copy(q, m):
        slab = (across, across, right, left, right, left)[m]
        side = (side_a, side_b, side_b, side_a, side_a, side_b)[m]
        to = (right, left)[m % 2]
        return remote(xs.at[q, slab, :, side], xr.at[q, m], x_s.at[m], x_r.at[q, min(m, 2)], dev(xx=to))

    def xphase(q):
        for m, slab, side in ((4, right, side_a), (5, left, side_b)):
            x_copy(q, m - 4).wait_recv()
            xs[q, slab, :, side] = (accf[q, slab, :, side] + xr[q, m - 4].astype(F32)).astype(BF16)
            x_copy(q, m).start()

    def z_send(q, d):
        to = (z + d) % NZ
        return remote(zs.at[q, to], zr.at[q, d - 1], z_s, z_r.at[q], dev(zz=to))

    def zphase(q):
        last = xr.at[q, 2:6]
        remote(last, last, x_s.at[2], x_r.at[q, 2], dev(xx=right)).wait_recv()
        value_a = accf[q, x, :, side_a] + xr[q, 4].astype(F32) + xr[q, 3].astype(F32)
        value_b = accf[q, x, :, side_b] + xr[q, 2].astype(F32) + xr[q, 5].astype(F32)
        for f in range(NF):
            join = fold_upper if f % 2 else fold
            at = slice(f // 2 * 8, f // 2 * 8 + 8)
            packed = jnp.concatenate(
                [join(v[at, :quarter], v[at, quarter:]) for v in (value_a, value_b)], axis=0)
            zsum[q, f] = packed
            zs[q, f] = packed.astype(BF16)
        for d in far_first(NZ):
            z_send(q, d).start()

    def y_send(n):
        return remote(ysend.at[n], yr.at[n], y_s, y_r.at[n], dev(hh=1 - yh))

    def yphase(q):
        remote(zr.at[q], zr.at[q], z_s, z_r.at[q], dev(zz=(z + 1) % NZ)).wait_recv()
        value = zsum[q, z]
        for d in range(NZ - 1):
            value = value + zr[q, d].astype(F32)
        n = q // 2

        @pl.when(yh == q % 2)
        def _():
            ykeep[n] = value

        @pl.when(yh != q % 2)
        def _():
            ysend[n] = value
            y_send(n).start()

    exchange_start(mf, feat, NF, mf_s, mf_r, at_f)
    ag_far(0)
    ag_near(0)
    ag_far(1)
    ag_near(1)
    ag_far(2)
    mz[z, :8, :] = mf[feat]
    exchange_wait(mf, feat, NF, mf_s, mf_r, at_f)
    for f in range(NF):
        mz[z, 8 + f : 9 + f, :] = mf[f, 0:1, :]
    exchange_start(mz, z, NZ, mz_s, mz_r, at_z)
    ag_near(2)
    ag_far(3)
    ag_near(3)
    exchange_wait(mz, z, NZ, mz_s, mz_r, at_z)
    mx[x] = slot_sum(mz, NZ)
    exchange_start(mx, x, NX, mx_s, mx_r, at_x)
    forward(0)
    forward(1)
    ag_far(4)
    ag_far(5)
    exchange_wait(mx, x, NX, mx_s, mx_r, at_x)
    my[yh] = slot_sum(mx, NX)
    exchange_start(my, yh, NYH, my_s, my_r, at_h)
    forward(2)
    forward(3)
    ag_near(4)
    ag_far(6)
    ag_far(7)
    share(0)
    exchange_wait(my, yh, NYH, my_s, my_r, at_h)
    mean = slot_sum(my, NYH) / total
    for i in range(8):
        mrow[:, 128 * i : 128 * (i + 1)] = mean[i : i + 1, :]

    def center(i, carry):
        at = pl.ds(pl.multiple_of(i * 64, 64), 64)
        cbuf[at, :] = (abuf[at, :].astype(F32) - mrow[...]).astype(BF16)
        return carry

    lax.fori_loop(0, tokens // 64, center, 0)
    forward(4)
    forward(5)
    ag_near(5)
    for f in range(NF):
        value = jnp.where(pick, mean[8 + f : 9 + f, :], 0.0)
        mcol[f] = jnp.broadcast_to(jnp.sum(value, axis=1, keepdims=True), (PANEL, PANEL))

    share(1)
    compute(0)
    xstart(0)
    forward(6)
    ag_near(6)
    ag_near(7)
    share(2)
    compute(1)
    xstart(1)
    share(3)
    compute(2)
    xphase(0)
    xstart(2)
    forward(7)
    share(4)
    compute(3)
    xphase(1)
    xstart(3)
    tags.wait()
    classes = lax.broadcasted_iota(jnp.int32, (16, tokens), 0)
    onehot = jnp.where(classes == labels_ref[...], 1.0, 0.0).astype(BF16)

    def class_columns(n, carry):
        at = pl.ds(pl.multiple_of(n * 256, 256), 256)
        part = jnp.dot(onehot, cbuf[:, at], preferred_element_type=F32)
        for k in range(CLASSES):
            for i in range(2):
                crs[k, pl.ds(2 * n + i, 1), :] = part[k : k + 1, 128 * i : 128 * (i + 1)]
        return carry

    lax.fori_loop(0, width // 256, class_columns, 0)
    crr[z] = crs[z]
    for d in far_first(NZ):
        to = (z + d) % NZ
        remote(crs.at[to], crr.at[z], cr_s, cr_r, at_z(to)).start()

    share(5)
    compute(4)
    xphase(2)
    xstart(4)
    zphase(0)
    compute(5)
    xphase(3)
    xstart(5)
    zphase(1)
    share(6)
    compute(6)
    xphase(4)
    xstart(6)
    zphase(2)
    share(7)
    exchange_wait(crr, z, NZ, cr_s, cr_r, at_z)
    cx[x] = slot_sum(crr, NZ)
    exchange_start(cx, x, NX, cx_s, cx_r, at_x)
    xphase(5)
    zphase(3)
    compute(7)
    xphase(6)
    zphase(4)
    exchange_wait(cx, x, NX, cx_s, cx_r, at_x)
    cy[yh] = slot_sum(cx, NX)
    exchange_start(cy, yh, NYH, cy_s, cy_r, at_h)
    yphase(0)
    yphase(1)
    zphase(5)
    xphase(7)
    zphase(6)
    yphase(2)
    zphase(7)
    exchange_wait(cy, yh, NYH, cy_s, cy_r, at_h)
    cg[z] = slot_sum(cy, NYH)
    exchange_start(cg, z, NZ, cg_s, cg_r, at_z)
    yphase(3)
    yphase(4)
    yphase(5)
    yphase(6)
    yphase(7)
    exchange_wait(cg, z, NZ, cg_s, cg_r, at_z)
    for k in range(CLASSES):
        for i in range(8):
            cross_ref[k : k + 1, 128 * i : 128 * (i + 1)] = cg[k, i : i + 1, :] / total
    cross_copy = pltpu.make_async_copy(cross_ref, cross_out, out_sem.at[2])
    cross_copy.start()
    cov_copies = []
    for n in range(Q // 2):
        y_send(n).wait_recv()
        value = (ykeep[n] + yr[n]) / (total - 1)
        for i in range(4):
            cov_ref[4 * n : 4 * n + 4, quarter * i : quarter * (i + 1)] = value[4 * i : 4 * i + 4, :]
        if n % 2:
            rows = pl.ds(4 * n - 4, 8)
            copy = pltpu.make_async_copy(cov_ref.at[rows], cov_out.at[rows], out_sem.at[n // 2])
            copy.start()
            cov_copies.append(copy)

    ag_drain()
    exchange_sent(mf, NF, mf_s, mf_r, at_f)
    exchange_sent(mz, NZ, mz_s, mz_r, at_z)
    exchange_sent(mx, NX, mx_s, mx_r, at_x)
    exchange_sent(my, NYH, my_s, my_r, at_h)
    exchange_sent(crr, NZ, cr_s, cr_r, at_z)
    exchange_sent(cx, NX, cx_s, cx_r, at_x)
    exchange_sent(cy, NYH, cy_s, cy_r, at_h)
    exchange_sent(cg, NZ, cg_s, cg_r, at_z)
    for m in range(6):
        sent = xr.at[:, m]
        remote(sent, sent, x_s.at[m], x_r.at[0, 0], dev(xx=right)).wait_send()
    remote(zr, zr, z_s, z_r.at[0], dev(zz=(z + 1) % NZ)).wait_send()
    remote(ysend, ysend, y_s, y_r.at[0], dev(hh=1 - yh)).wait_send()
    for copy in cov_copies:
        copy.wait()
    cross_copy.wait()

def body(activations, labels):
    tokens, width = activations.shape
    out_rows = NF * PANEL // (NZ * NYH * NX)
    dma = pltpu.SemaphoreType.DMA
    vm = pltpu.VMEM
    tile = (8, 128)
    scratch = [
        vm((tokens, width), BF16),
        vm((1, tokens), jnp.int32),
        vm((tokens, width), BF16),
        vm((Q, NC, NY, ROWS, tokens), BF16),
        vm((NF * ROWS, tokens), BF16),
        vm((Q, NX, NF * 4, width), F32),
        vm((Q, NX, NF * 4, width), BF16),
        vm((Q, 6, NF * 4, width // 2), BF16),
        vm((Q, NF, 16, width // 4), F32),
        vm((Q, NZ, 16, width // 4), BF16),
        vm((Q, NZ - 1, 16, width // 4), BF16),
        vm((Q // 2, 16, width // 4), F32),
        vm((Q // 2, 16, width // 4), F32),
        vm((Q // 2, 16, width // 4), F32),
        vm((NZ, 16, 128), F32),
        vm((NX, 16, 128), F32),
        vm((NYH, 16, 128), F32),
        vm((NF, *tile), F32),
        vm((1, width), F32),
        vm((NF, PANEL, PANEL), F32),
        vm((CLASSES, *tile), F32),
        vm((NZ, *tile), F32),
        vm((NX, *tile), F32),
        vm((NYH, *tile), F32),
        vm((NZ, *tile), F32),
        vm((out_rows, width), F32),
        vm((CLASSES, width), F32),
        dma((3,)),
        dma((3,)),
        dma((Q, NY)), dma((Q,)), dma((6,)),
        dma((6,)), dma((Q, 3)),
        dma(()), dma((Q,)),
        dma(()), dma((Q // 2,)),
    ] + [dma(())] * 16
    return pl.pallas_call(
        kernel,
        out_shape=(
            jax.ShapeDtypeStruct((out_rows, width), F32),
            jax.ShapeDtypeStruct((CLASSES, width), F32),
        ),
        in_specs=[
            pl.BlockSpec(memory_space=pl.ANY),
            pl.BlockSpec(memory_space=pl.ANY),
        ],
        out_specs=(
            pl.BlockSpec(memory_space=pl.ANY),
            pl.BlockSpec(memory_space=pl.ANY),
        ),
        scratch_shapes=scratch,
        compiler_params=pltpu.CompilerParams(
            collective_id=0, has_side_effects=True, vmem_limit_bytes=60 * 2**20
        ),
        name="stats",
    )(activations, labels.reshape(1, tokens))


def solution(mesh):
    in_specs = (P("tok", "feat"), P("tok"))
    out_specs = (P("tok", "feat"), P(None, "feat"))
    return jax.shard_map(body, mesh=mesh, in_specs=in_specs, out_specs=out_specs, check_vma=False)
```
